512 devices in a mesh: dp: 64 (over x, y_hi, z), tensor: 8 (over y_lo, core).
Axes of the slice: x: 4, y: 8 (y_hi: 2, y_lo: 4; y = y_hi * 4 + y_lo), z: 8, core: 2. Of those that a mesh axis runs over, the one named last changes fastest.
Arguments:
- frames_in: bfloat16 [64, 1024, 1536], P('dp', 'tensor'), may hold values from -6 to 6
- lengths: int32 [64], P('dp'), may hold values from 341 to 1024, as said below
- ln_gain: float32 [1536], replicated, may hold values from 0.5 to 2
- ln_bias: float32 [1536], replicated, may hold values from -3 to 3
- glu_weight: bfloat16 [2, 1536, 1536], P(None, 'tensor'), may hold values from -0.15625 to 0.15625
- conv_kernel: bfloat16 [32, 1536], P(None, 'tensor'), may hold values from -1 to 1
- bn_gain: float32 [1536], P('tensor'), may hold values from 0.5 to 2
- bn_bias: float32 [1536], P('tensor'), may hold values from -3 to 3
- out_weight: bfloat16 [1536, 1536], P('tensor'), may hold values from -0.15625 to 0.15625
Outputs:
- frames_out: bfloat16 [64, 1024, 1536], P('dp', 'tensor')
The draws below stay inside these ranges and needn't reach their ends.
Inputs may be any that keep to these rules, and one draw needn't show every extreme that they name: `lengths`: each span's length lies between 341 and 1024; some span is full in every draw.
All inputs are finite; a program needn't handle non-finite values.
Results may differ from the reference program's by a relative error of at most 0.0095.
Values may be sent and summed in bfloat16 or wider, within the bound.
A program may use at most 64 MiB of HBM per device.

```python
import math
import jax
import jax.numpy as jnp
from jax import lax

D = 1536
KERNEL = 32
FRAMES = 1024
SPANS = 64


def draw_lengths(key, part):
    index = jnp.arange(SPANS, dtype=jnp.int32)
    low = FRAMES // 3
    base = low + index * (FRAMES - low) // max(SPANS - 1, 1)
    jitter = jax.random.randint(key, (SPANS,), 0, FRAMES // 8 + 1)
    values = jnp.minimum(base + jitter, FRAMES)
    where_full = jax.random.randint(jax.random.fold_in(key, 7), (), 0, SPANS)
    return values.at[where_full].set(FRAMES).astype(jnp.int32)


def draw_frames_in(key, part):
    key_base = jax.random.fold_in(key, 11)
    key_gain = jax.random.fold_in(key, 12)
    key_offset = jax.random.fold_in(key, 13)
    base = jax.random.normal(key_base, (SPANS, FRAMES, D), jnp.float32)
    spread = 0.7
    shift = 0.5
    gains = jnp.exp(jax.random.uniform(key_gain, (SPANS, 1, D), jnp.float32, -spread, spread))
    offsets = shift * jax.random.normal(key_offset, (SPANS, 1, D), jnp.float32)
    values = jnp.clip(base * gains + offsets, -6.0, 6.0)
    return values.astype(jnp.bfloat16)


def level_of(key, dims, split, least, high):
    def one(dim, blocks):
        steps = jax.random.uniform(jax.random.fold_in(jax.random.fold_in(key, 6), dim), (blocks,), jnp.float32, least / len(split), high / len(split))
        return jnp.repeat(jnp.exp(steps), dims[dim] // blocks).reshape((-1,) + (1,) * (len(dims) - dim - 1))

    loudness = one(*split[0])
    for cut in split[1:]:
        loudness = loudness * one(*cut)
    return loudness


def bell_draw(key, extent, deviation, most, pieces=(), kind=jnp.bfloat16):
    drawn = jax.random.normal(key, extent, jnp.float32) * deviation
    if len(pieces) > 0:
        drawn = level_of(key, extent, pieces, -0.22, 0.18) * drawn
    return jnp.clip(drawn, min=-most, max=most).astype(kind)


def setup_inputs(seed: int = 0) -> dict:
    arg_keys = jax.random.split(jax.random.key(seed), 10)
    frames_in = draw_frames_in(jax.random.fold_in(arg_keys[9], 71), 0)
    lengths = draw_lengths(jax.random.fold_in(arg_keys[9], 71), 0)
    ln_gain = jnp.clip(jnp.exp(jax.random.uniform(arg_keys[2], (D,), jnp.float32, math.log(0.5), math.log(2.0))), 0.5, 2.0)
    ln_bias = bell_draw(arg_keys[3], (D,), 0.5, 3.0, (), jnp.float32)
    glu_weight = bell_draw(arg_keys[4], (2, D, D), D ** -0.5, 0.15625, ((1, 8),))
    conv_kernel = bell_draw(arg_keys[5], (KERNEL, D), KERNEL ** -0.5, 1.0, ((1, 8),))
    bn_gain = jnp.clip(jnp.exp(math.log(2.0) - 1.3862944 * jax.random.uniform(arg_keys[6], (D,), jnp.float32) ** level_of(arg_keys[6], (D,), ((0, 8),), -0.2, 0.2)), 0.5, 2.0)
    bn_bias = bell_draw(arg_keys[7], (D,), 0.5, 3.0, ((0, 8),), jnp.float32)
    out_weight = bell_draw(arg_keys[8], (D, D), D ** -0.5, 0.15625, ((0, 8),))
    return {"frames_in": frames_in, "lengths": lengths, "ln_gain": ln_gain, "ln_bias": ln_bias, "glu_weight": glu_weight, "conv_kernel": conv_kernel, "bn_gain": bn_gain, "bn_bias": bn_bias, "out_weight": out_weight}


def layer_norm(rows, gain, bias):
    values = rows.astype(jnp.float32)
    center = lax.optimization_barrier(jnp.mean(values, axis=-1, keepdims=True))
    spread = lax.optimization_barrier(jnp.mean((values - center) ** 2, axis=-1, keepdims=True))
    return ((values - center) * lax.rsqrt(spread + 1e-05) * gain + bias).astype(jnp.bfloat16)

def span_conv(item, ln_gain, ln_bias, glu_weight, conv_kernel):
    rows, length = item
    normed = layer_norm(rows, ln_gain, ln_bias)
    value = jnp.dot(normed, glu_weight[0].T, preferred_element_type=jnp.float32)
    gate = jnp.dot(normed, glu_weight[1].T, preferred_element_type=jnp.float32)
    glu = (value * jax.nn.sigmoid(gate)).astype(jnp.bfloat16)
    valid = jnp.arange(rows.shape[0], dtype=jnp.int32) < length
    glu = jnp.where(valid[:, None], glu, jnp.zeros_like(glu)).astype(jnp.float32)
    padded = jnp.pad(glu, ((15, KERNEL - 16), (0, 0)))
    taps = conv_kernel.astype(jnp.float32)
    total = jnp.zeros_like(glu)
    for k in range(KERNEL):
        total = total + padded[k:k + rows.shape[0]] * taps[k]
    return total

def reference(frames_in, lengths, ln_gain, ln_bias, glu_weight, conv_kernel, bn_gain, bn_bias, out_weight):
    conv = lax.map(lambda item: span_conv(item, ln_gain, ln_bias, glu_weight, conv_kernel), (frames_in, lengths))
    valid = (jnp.arange(FRAMES, dtype=jnp.int32)[None, :] < lengths[:, None]).astype(jnp.float32)[:, :, None]
    count = jnp.sum(lengths.astype(jnp.float32))
    mean = lax.optimization_barrier(jnp.sum(conv * valid, axis=(0, 1))) / count
    var = lax.optimization_barrier(jnp.sum(((conv - mean) * valid) ** 2, axis=(0, 1))) / count
    scale = lax.rsqrt(var + 1e-05) * bn_gain

    def finish(item):
        rows, conv_rows = item
        z = (conv_rows - mean) * scale + bn_bias
        act = (z * jax.nn.sigmoid(z)).astype(jnp.bfloat16)
        branch = jnp.dot(act, out_weight.T, preferred_element_type=jnp.float32)
        return (rows.astype(jnp.float32) + branch).astype(jnp.bfloat16)
    return lax.map(finish, (frames_in, conv))
```

```python
import functools

import jax
import jax.numpy as jnp
from jax import lax
from jax.experimental import pallas as pl
from jax.experimental.pallas import tpu as pltpu
from jax.sharding import PartitionSpec as P

MESH = pl.DeviceIdType.MESH
F32 = jnp.float32
BF16 = jnp.bfloat16
TAPS = 32
D = 1536
SHARD = 192
CHIP = 384
ROWS = 128
HALO = 16
SPAN = 2 * ROWS
WIN = SPAN + 2 * HALO
PIECES = 3
PROWS = SHARD // PIECES
WCH = 6
WROWS = SHARD // WCH

NAMES = (
    ["glu_sib"]
    + [f"glu_x{i}" for i in range(PIECES)]
    + [f"glu_f{i}" for i in range(PIECES)]
    + ["blk0", "blk1", "low", "high"]
    + ["pack_s", "pack_e", "pack_d"]
    + ["w_sib", "w_par", "w_fp"]
    + [f"w_e{i}" for i in range(WCH)]
    + [f"w_ep{i}" for i in range(WCH)]
    + [f"w_fe{i}" for i in range(WCH)]
    + [f"w_fep{i}" for i in range(WCH)]
    + [f"d{k}_{g}" for k in range(3) for g in range(2)]
    + ["ml0", "ml1"]
)
SEM = {name: i for i, name in enumerate(NAMES)}
SENDS = NAMES + ["blk_s", "blk_p", "low1", "high1"]
SSEM = {name: i for i, name in enumerate(SENDS)}


def body(
    frames, lengths, ln_gain, ln_bias, glu_w, taps_in, bn_gain, bn_bias, out_w, out,
    xin, lng, lnb, tin, bg, bb, own, nbuf, wg, wf, pack, par, gs, cv, dsend, dbuf,
    msg, plane, bmsg, gmsg, ball, gall, mlx, act,
    lsem, ssem, rsem, asend, arecv, bsend, brecv, gsend, grecv,
):
    dp = lax.axis_index("dp")
    t = lax.axis_index("tensor")
    x, yh, z = dp // 16, (dp // 8) % 2, dp % 8
    y, c = t // 2, t % 2
    h, j = y // 2, y % 2
    me = yh * 8 + t
    sib = t + 1 - 2 * c
    par_t = (y + 1 - 2 * j) * 2 + c
    ext_t = (3 - y) * 2 + c
    ext_s = (3 - y) * 2 + 1 - c
    edge = (y == 0) | (y == 3)
    ext_dp = jnp.where(edge, dp + 8 - 16 * yh, dp)
    pe_t = (3 - (y + 1 - 2 * j)) * 2 + c

    def rcopy(src, dst, send, recv, tensor, to_dp=dp):
        return pltpu.make_async_remote_copy(
            src_ref=src, dst_ref=dst, send_sem=ssem.at[SSEM[send]], recv_sem=rsem.at[SEM[recv]],
            device_id={"dp": to_dp, "tensor": tensor}, device_id_type=MESH,
        )

    def arrived(dst, recv):
        pltpu.make_async_remote_copy(
            src_ref=dst, dst_ref=dst, send_sem=ssem.at[0], recv_sem=rsem.at[SEM[recv]],
            device_id={"dp": dp, "tensor": sib}, device_id_type=MESH,
        ).wait_recv()

    barrier = pltpu.get_barrier_semaphore()

    def greet_plane(i, _):
        to = (((x + i // 8) % 4) * 2 + yh) * 8 + (z + i % 8) % 8
        pl.semaphore_signal(barrier, inc=1, device_id={"dp": to, "tensor": t}, device_id_type=MESH)
        return 0

    def greet_line(i, _):
        q = (me + i) % 16
        to = (x * 2 + q // 8) * 8 + z
        pl.semaphore_signal(barrier, inc=1, device_id={"dp": to, "tensor": q % 8}, device_id_type=MESH)
        return 0

    lax.fori_loop(1, 16, greet_line, 0)
    lax.fori_loop(1, 32, greet_plane, 0)

    loads = [
        pltpu.make_async_copy(frames.at[0], xin, lsem.at[0]),
        pltpu.make_async_copy(ln_gain, lng, lsem.at[1]),
        pltpu.make_async_copy(ln_bias, lnb, lsem.at[2]),
        pltpu.make_async_copy(taps_in, tin, lsem.at[3]),
        pltpu.make_async_copy(bn_gain, bg, lsem.at[4]),
        pltpu.make_async_copy(bn_bias, bb, lsem.at[5]),
        pltpu.make_async_copy(glu_w, wg.at[h, :, pl.ds(pl.multiple_of(SHARD * c, 64), SHARD)], lsem.at[6]),
        pltpu.make_async_copy(out_w, wf.at[pl.ds(pl.multiple_of(SHARD * t, 64), SHARD)], lsem.at[7]),
    ]
    for copy in loads:
        copy.start()
    for copy in loads[:6]:
        copy.wait()

    rows = xin[...].astype(F32)
    center = jnp.mean(rows, axis=-1, keepdims=True)
    spread = jnp.mean((rows - center) ** 2, axis=-1, keepdims=True)
    own[...] = ((rows - center) * lax.rsqrt(spread + 1e-05) * lng[...] + lnb[...]).astype(BF16)

    pack[0] = jnp.zeros_like(pack[0])
    pack[0, 0:TAPS, 0:SHARD] = tin[...].astype(F32)
    pack[0, TAPS : TAPS + 1, 0:SHARD] = bg[...]
    pack[0, TAPS + 1 : TAPS + 2, 0:SHARD] = bb[...]

    same = (y + 2 * c - 1) // 2 == h
    gives = ((c == 1) & (y < 3)) | ((c == 0) & (y > 0))
    y2 = y + 2 * c - 1
    h2, j2 = y2 // 2, (y2 + 2) % 2
    mine = j == c

    @pl.when(mine)
    def _():
        nbuf[pl.ds(pl.multiple_of(HALO + ROWS * c, 16), ROWS), :] = own[...]

    @pl.when((c == 1) & (j == 0))
    def _():
        nbuf[0:HALO, :] = own[ROWS - HALO : ROWS, :]

    @pl.when((c == 0) & (j == 1))
    def _():
        nbuf[WIN - HALO : WIN, :] = own[0:HALO, :]

    @pl.when((c == 0) & (h == 0))
    def _():
        nbuf[0:HALO, :] = jnp.zeros((HALO, D), BF16)

    @pl.when((c == 1) & (h == 1))
    def _():
        nbuf[WIN - HALO : WIN, :] = jnp.zeros((HALO, D), BF16)

    pl.semaphore_wait(barrier, 46)

    def glu_rows(slot, core, i):
        first = SHARD * core + PROWS * jnp.where(core == 0, i, PIECES - 1 - i)
        return wg.at[slot, :, pl.ds(pl.multiple_of(first, 64), PROWS)]

    glu_x = []
    for i in range(PIECES):
        first = PROWS * jnp.where(c == 0, i, PIECES - 1 - i)
        src = glu_w.at[:, pl.ds(pl.multiple_of(first, 64), PROWS)]
        glu_x.append(rcopy(src, glu_rows(h, c, i), f"glu_x{i}", f"glu_x{i}", ext_t, ext_dp))
        glu_x[-1].start()

    spot = nbuf.at[pl.ds(pl.multiple_of(HALO + ROWS * c, 16), ROWS)]

    def block_to(send, tensor):
        return (
            rcopy(own, spot, send, "blk0", tensor),
            rcopy(own, spot, send, "blk1", tensor),
        )

    to_partner = block_to("blk_p", (y + 1 - 2 * j) * 2 + j)
    to_sibling = block_to("blk_s", sib)
    for core in range(2):
        pl.when(c == core)(to_partner[core].start)
        pl.when((c == core) & jnp.logical_not(mine))(to_sibling[core].start)

    low = nbuf.at[0:HALO]
    high = nbuf.at[WIN - HALO : WIN]
    tail = own.at[ROWS - HALO : ROWS]
    head = own.at[0:HALO]
    halo_a = jnp.where(same, par_t, (2 * h2) * 2 + j2)
    halo_b = (2 * h2 + 1) * 2 + j2
    halos = [
        ((c == 1) & gives, rcopy(tail, low, "low", "low", halo_a)),
        ((c == 1) & gives & jnp.logical_not(same), rcopy(tail, low, "low1", "low", halo_b)),
        ((c == 0) & gives, rcopy(head, high, "high", "high", halo_a)),
        ((c == 0) & gives & jnp.logical_not(same), rcopy(head, high, "high1", "high", halo_b)),
    ]
    for cond, copy in halos:
        pl.when(cond)(copy.start)

    glu_sib = rcopy(
        glu_w, wg.at[h, :, pl.ds(pl.multiple_of(SHARD * c, 64), SHARD)], "glu_sib", "glu_sib", sib
    )
    glu_sib.start()
    packs = [
        rcopy(pack.at[0], pack.at[1], "pack_s", "pack_s", sib),
        rcopy(pack.at[0], pack.at[2], "pack_e", "pack_e", ext_t, ext_dp),
        rcopy(pack.at[0], pack.at[3], "pack_d", "pack_d", ext_s, ext_dp),
    ]
    for copy in packs:
        copy.start()

    def w_rows(shard, first=0, n=SHARD):
        return wf.at[pl.ds(pl.multiple_of(SHARD * shard + first, 32), n)]

    w_sib = rcopy(out_w, w_rows(t), "w_sib", "w_sib", sib)
    w_sib.start()

    lane = lax.broadcasted_iota(jnp.int32, (40, 128), 1)

    def tiles_of(slot, mine_at, other_at):
        a = pack[mine_at]
        b = pack[other_at]
        first = jnp.where(c == 0, a, b)
        second = jnp.where(c == 0, b, a)
        r0 = pltpu.roll(second[:, 0:128], 64, 1)
        r1 = pltpu.roll(second[:, 128:256], 64, 1)
        par[3 * slot] = first[:, 0:128]
        par[3 * slot + 1] = jnp.where(lane < 64, first[:, 128:256], r0)
        par[3 * slot + 2] = jnp.where(lane < 64, r0, r1)

    arrived(pack.at[1], "pack_s")
    tiles_of(h, 0, 1)
    arrived(pack.at[2], "pack_e")
    arrived(pack.at[3], "pack_d")
    tiles_of(1 - h, 2, 3)
    gmsg[...] = jnp.zeros_like(gmsg)
    for k in range(6):
        gmsg[k : k + 1, :] = par[k, TAPS : TAPS + 1, :]
        gmsg[8 + k : 9 + k, :] = par[k, TAPS + 1 : TAPS + 2, :]

    def line(i, src, dst, ss, rs):
        q = (me + i) % 16
        to = (x * 2 + q // 8) * 8 + z
        return pltpu.make_async_remote_copy(
            src_ref=src, dst_ref=dst.at[me], send_sem=ss.at[i], recv_sem=rs.at[me],
            device_id={"dp": to, "tensor": q % 8}, device_id_type=MESH,
        )

    def send_gains(i, _):
        line(i, gmsg, gall, gsend, grecv).start()
        return 0

    lax.fori_loop(1, 16, send_gains, 0)

    length = lengths[0]
    start = 2 * SPAN * h + SPAN * c
    count = jnp.clip(length - start, 0, SPAN)
    count_f = count.astype(F32)
    inverse = 1.0 / jnp.maximum(count_f, 1.0)
    msg[...] = jnp.zeros_like(msg)
    msg[6:7, :] = jnp.full((1, 128), count_f, F32)

    def one_tile(slot, q):
        k = 3 * slot + q
        w = wg[slot, :, pl.ds(pl.multiple_of(128 * q, 128), 128), :].reshape(256, D)
        both = lax.dot_general(nbuf[...], w, (((1,), (1,)), ((), ())), preferred_element_type=F32)
        glu = (both[:, 0:128] * jax.nn.sigmoid(both[:, 128:256])).astype(BF16).astype(F32)
        at = lax.broadcasted_iota(jnp.int32, (WIN, 128), 0)
        gs[...] = jnp.where(at < length - start + HALO, glu, 0.0)
        step = 64

        def conv_rows(i, total):
            first = pl.multiple_of(i * step, step)
            acc = jnp.zeros((step, 128), F32)
            for tap in range(TAPS):
                acc = acc + gs[pl.ds(first + (tap + 1), step), :] * par[k, tap : tap + 1, :]
            cv[pl.ds(first, step), :] = acc
            here = first + lax.broadcasted_iota(jnp.int32, (step, 128), 0)
            kept = jnp.where(here < count, acc, 0.0)
            return total + jnp.sum(kept.reshape(step // 8, 8, 128), axis=0)

        total = lax.fori_loop(0, SPAN // step, conv_rows, jnp.zeros((8, 128), F32))
        local = jnp.sum(total, axis=0, keepdims=True) * inverse
        dev = cv[...] - local
        dsend[k] = dev.astype(BF16)
        here = lax.broadcasted_iota(jnp.int32, (SPAN, 128), 0)
        kept = jnp.where(here < count, dev, 0.0)
        msg[pl.ds(k, 1), :] = local
        msg[pl.ds(8 + k, 1), :] = jnp.sum(kept * kept, axis=0, keepdims=True)

    owner = 2 * (2 * h + c)
    shard_of = (jnp.minimum(y, 3 - y), jnp.maximum(y, 3 - y))

    def give(slot, q, n, group):
        base = 3 * jnp.where(slot == 0, shard_of[0], shard_of[1]) + q
        copies = []
        for g in range(2):
            src = dsend.at[pl.ds(3 * slot + q, n), pl.ds(ROWS * g, ROWS)]
            dst = dbuf.at[pl.ds(base, n)]
            name = f"d{group}_{g}"
            away = [
                (jnp.logical_not(mine & (c == g)) & (j == s),
                 rcopy(src, dst, name, f"d{group}_{s}", owner + g))
                for s in range(2)
            ]
            for cond, copy in away:
                pl.when(cond)(copy.start)
                copies.append((cond, copy))

            @pl.when(mine & (c == g))
            def _(src=src, dst=dst):
                keep = pltpu.make_async_copy(src, dst, lsem.at[8])
                keep.start()
                keep.wait()
        return copies

    for p in range(2):
        @pl.when(jnp.logical_not(mine & (c == p)))
        def _(p=p):
            arrived(nbuf.at[HALO + ROWS * p : HALO + ROWS * (p + 1)], f"blk{p}")

    @pl.when(((c == 1) & (j == 1)) | ((c == 0) & (h == 1)))
    def _():
        arrived(low, "low")

    @pl.when(((c == 0) & (j == 0)) | ((c == 1) & (h == 0)))
    def _():
        arrived(high, "high")

    loads[6].wait()
    arrived(wg.at[h, :, pl.ds(pl.multiple_of(SHARD * (1 - c), 64), SHARD)], "glu_sib")

    w_par = rcopy(out_w, w_rows(t), "w_par", "w_par", par_t)
    w_par.start()

    def own_tile(q, _):
        one_tile(h, q)
        return 0

    lax.fori_loop(0, 3, own_tile, 0)
    given = give(h, 0, 3, 0)

    glu_f = []
    for i in range(2):
        arrived(glu_rows(1 - h, c, i), f"glu_x{i}")
        glu_f.append(rcopy(glu_rows(1 - h, c, i), glu_rows(1 - h, c, i), f"glu_f{i}", f"glu_f{i}", sib))
        glu_f[-1].start()
    for i in range(2):
        arrived(glu_rows(1 - h, 1 - c, i), f"glu_f{i}")

    def extra_tile(i, _):
        one_tile(1 - h, 2 * i)
        return 0

    lax.fori_loop(0, 2, extra_tile, 0)
    given += give(1 - h, 0, 1, 1)
    arrived(w_rows(par_t), "w_par")
    w_fp = rcopy(w_rows(par_t), w_rows(par_t), "w_fp", "w_fp", sib)
    w_fp.start()

    arrived(glu_rows(1 - h, c, 2), "glu_x2")
    glu_f.append(rcopy(glu_rows(1 - h, c, 2), glu_rows(1 - h, c, 2), "glu_f2", "glu_f2", sib))
    glu_f[-1].start()
    w_e = []
    for i in range(WCH):
        w_e.append(rcopy(
            out_w.at[pl.ds(WROWS * i, WROWS)], w_rows(t, WROWS * i, WROWS), f"w_e{i}", f"w_e{i}", ext_t, ext_dp
        ))
        w_e[-1].start()
    arrived(glu_rows(1 - h, 1 - c, 2), "glu_f2")
    one_tile(1 - h, 1)

    def plane_copy(i):
        to = (((x + i // 8) % 4) * 2 + yh) * 8 + (z + i % 8) % 8
        return pltpu.make_async_remote_copy(
            src_ref=msg, dst_ref=plane.at[i], send_sem=asend.at[i], recv_sem=arecv.at[i],
            device_id={"dp": to, "tensor": t}, device_id_type=MESH,
        )

    def send_plane(i, _):
        plane_copy(i).start()
        return 0

    lax.fori_loop(1, 32, send_plane, 0)
    given += give(1 - h, 1, 2, 2)
    u = jnp.where(edge, 0, 1)
    means = []
    for g in range(2):
        away = [
            (jnp.logical_not(mine & (c == g)) & (u == s),
             rcopy(msg.at[0:8], mlx.at[s], f"ml{g}", f"ml{s}", owner + g))
            for s in range(2)
        ]
        for cond, copy in away:
            pl.when(cond)(copy.start)
            means.append((cond, copy))

    @pl.when(mine)
    def _():
        mlx[u] = msg[0:8, :]

    w_fwd = []

    def forward(i):
        at = w_rows(ext_t, WROWS * i, WROWS)
        arrived(at, f"w_e{i}")
        for name, to in ((f"w_ep{i}", par_t), (f"w_fe{i}", sib)):
            copy = rcopy(at, at, name, name, to)
            copy.start()
            w_fwd.append(copy)

    def forward_again(i):
        at = w_rows(pe_t, WROWS * i, WROWS)
        arrived(at, f"w_ep{i}")
        copy = rcopy(at, at, f"w_fep{i}", f"w_fep{i}", sib)
        copy.start()
        w_fwd.append(copy)

    def merge(blocks):
        n = sum(jnp.broadcast_to(b[6:7, :], (8, 128)) for b in blocks)
        weighted = sum(jnp.broadcast_to(b[6:7, :], (8, 128)) * b[0:8, :] for b in blocks)
        mean = weighted / jnp.maximum(n, 1.0)
        square = sum(
            b[8:16, :] + jnp.broadcast_to(b[6:7, :], (8, 128)) * (b[0:8, :] - mean) ** 2 for b in blocks
        )
        return n, mean, square

    for i in range(3):
        forward(i)

    def wait_plane(i, _):
        plane_copy(i).wait_recv()
        return 0

    lax.fori_loop(1, 32, wait_plane, 0)
    plane[0] = msg[...]
    n, mean, square = merge([plane[i] for i in range(32)])
    row = lax.broadcasted_iota(jnp.int32, (8, 128), 0)
    bmsg[0:8, :] = jnp.where(row == 6, n, mean)
    bmsg[8:16, :] = square

    def send_line(i, _):
        line(i, bmsg, ball, bsend, brecv).start()
        return 0

    lax.fori_loop(1, 16, send_line, 0)
    ball[me] = bmsg[...]
    gall[me] = gmsg[...]

    for i in range(3, WCH):
        forward(i)
        forward_again(i - 3)

    def wait_line(i, _):
        q = (me + i) % 16
        for dst, rs in ((ball, brecv), (gall, grecv)):
            pltpu.make_async_remote_copy(
                src_ref=bmsg, dst_ref=dst.at[q], send_sem=bsend.at[0], recv_sem=rs.at[q],
                device_id={"dp": dp, "tensor": sib}, device_id_type=MESH,
            ).wait_recv()
        return 0

    lax.fori_loop(1, 16, wait_line, 0)

    for group, n in ((0, 3), (1, 1), (2, 2)):
        for s in range(2):
            @pl.when(jnp.logical_not((j == s) & mine))
            def _(group=group, n=n, s=s):
                arrived(dbuf.at[pl.ds(0, n)], f"d{group}_{s}")
    for s in range(2):
        @pl.when(jnp.logical_not((u == s) & mine))
        def _(s=s):
            arrived(mlx.at[s], f"ml{s}")

    sets = ((0, 1, 6, 7), (2, 3, 4, 5))
    offset, scale, shift = [], [], []
    for s in range(2):
        n, mean, square = merge([ball[8 * g + q] for g in range(2) for q in sets[s]])
        n1 = jnp.broadcast_to(n[0:1, :], (8, 128))
        gains = gall[sets[s][0]]
        offset.append(mlx[s] - mean)
        scale.append(lax.rsqrt(square / n1 + 1e-05) * gains[0:8, :])
        shift.append(gains[8:16, :])
    where = [(0, 0), (0, 1), (0, 2), (1, 0), (1, 1), (1, 2), (1, 3), (1, 4), (1, 5), (0, 3), (0, 4), (0, 5)]
    for g, (s, r) in enumerate(where):
        zed = (dbuf[g].astype(F32) + offset[s][r : r + 1, :]) * scale[s][r : r + 1, :] + shift[s][r : r + 1, :]
        act[:, 128 * g : 128 * (g + 1)] = (zed * jax.nn.sigmoid(zed)).astype(BF16)

    for i in range(3, WCH):
        forward_again(i)
    loads[7].wait()
    arrived(w_rows(sib), "w_sib")
    arrived(w_rows(par_t + 1 - 2 * c), "w_fp")
    for i in range(WCH):
        arrived(w_rows(ext_s, WROWS * i, WROWS), f"w_fe{i}")
    for i in range(WCH):
        arrived(w_rows(pe_t + 1 - 2 * c, WROWS * i, WROWS), f"w_fep{i}")

    def columns(i, _):
        at = pl.multiple_of(256 * i, 256)
        branch = lax.dot_general(
            act[...], wf[pl.ds(at, 256), :], (((1,), (1,)), ((), ())), preferred_element_type=F32
        )
        out[0, :, pl.ds(at, 256)] = (xin[:, pl.ds(at, 256)].astype(F32) + branch).astype(BF16)
        return 0

    lax.fori_loop(0, D // 256, columns, 0)

    for copy in glu_x + [glu_sib] + packs + [w_sib, w_par, w_fp] + glu_f + w_e + w_fwd:
        copy.wait_send()
    for core in range(2):
        pl.when(c == core)(to_partner[core].wait_send)
        pl.when((c == core) & jnp.logical_not(mine))(to_sibling[core].wait_send)
    for cond, copy in halos + given + means:
        pl.when(cond)(copy.wait_send)

    def sent_plane(i, _):
        plane_copy(i).wait_send()
        return 0

    def sent_line(i, _):
        line(i, bmsg, ball, bsend, brecv).wait_send()
        line(i, gmsg, gall, gsend, grecv).wait_send()
        return 0

    lax.fori_loop(1, 32, sent_plane, 0)
    lax.fori_loop(1, 16, sent_line, 0)


def per_device(
    frames_in, lengths, ln_gain, ln_bias, glu_weight, conv_kernel, bn_gain, bn_bias, out_weight
):
    hbm = pl.BlockSpec(memory_space=pl.ANY)
    dma = pltpu.SemaphoreType.DMA
    return pl.pallas_call(
        body,
        out_shape=jax.ShapeDtypeStruct((1, ROWS, D), BF16),
        in_specs=[hbm, pl.BlockSpec(memory_space=pltpu.SMEM)] + [hbm] * 7,
        out_specs=pl.BlockSpec(memory_space=pltpu.VMEM),
        scratch_shapes=[
            pltpu.VMEM((ROWS, D), BF16),
            pltpu.VMEM((1, D), F32),
            pltpu.VMEM((1, D), F32),
            pltpu.VMEM((TAPS, SHARD), BF16),
            pltpu.VMEM((1, SHARD), F32),
            pltpu.VMEM((1, SHARD), F32),
            pltpu.VMEM((ROWS, D), BF16),
            pltpu.VMEM((WIN, D), BF16),
            pltpu.VMEM((2, 2, CHIP, D), BF16),
            pltpu.VMEM((D, D), BF16),
            pltpu.VMEM((4, 40, 256), F32),
            pltpu.VMEM((6, 40, 128), F32),
            pltpu.VMEM((WIN, 128), F32),
            pltpu.VMEM((SPAN, 128), F32),
            pltpu.VMEM((6, SPAN, 128), BF16),
            pltpu.VMEM((12, ROWS, 128), BF16),
            pltpu.VMEM((16, 128), F32),
            pltpu.VMEM((32, 16, 128), F32),
            pltpu.VMEM((16, 128), F32),
            pltpu.VMEM((16, 128), F32),
            pltpu.VMEM((16, 16, 128), F32),
            pltpu.VMEM((16, 16, 128), F32),
            pltpu.VMEM((2, 8, 128), F32),
            pltpu.VMEM((ROWS, D), BF16),
            dma((9,)),
            dma((len(SENDS),)),
            dma((len(NAMES),)),
            dma((32,)),
            dma((32,)),
            dma((16,)),
            dma((16,)),
            dma((16,)),
            dma((16,)),
        ],
        compiler_params=pltpu.CompilerParams(
            collective_id=0, has_side_effects=True, vmem_limit_bytes=48 << 20
        ),
    )(
        frames_in, lengths, ln_gain.reshape(1, D), ln_bias.reshape(1, D), glu_weight, conv_kernel,
        bn_gain.reshape(1, SHARD), bn_bias.reshape(1, SHARD), out_weight,
    )


def solution(mesh):
    return jax.shard_map(
        per_device,
        mesh=mesh,
        in_specs=(
            P("dp", "tensor", None),
            P("dp"),
            P(),
            P(),
            P(None, "tensor", None),
            P(None, "tensor"),
            P("tensor"),
            P("tensor"),
            P("tensor", None),
        ),
        out_specs=P("dp", "tensor", None),
        check_vma=False,
    )
```

```python
import functools

import jax
import jax.numpy as jnp
from jax import lax
from jax.experimental import pallas as pl
from jax.experimental.pallas import tpu as pltpu
from jax.sharding import PartitionSpec as P

MESH = pl.DeviceIdType.MESH
F32 = jnp.float32
BF16 = jnp.bfloat16
TAPS = 32
D = 1536
SHARD = 192
CHIP = 384
ROWS = 128
HALO = 16
SPAN = 2 * ROWS
WIN = SPAN + 2 * HALO
QUARTER = SHARD // 4
CHUNKS = 3
CROWS = QUARTER // CHUNKS
SENDS = 128

NAMES = (
    ["glu_sib", "blk0", "blk1", "low", "high", "pack_s", "pack_e", "pack_d", "w_sib"]
    + [f"gy{i}" for i in range(CHUNKS)]
    + [f"gx{k}_{i}" for k in range(3) for i in range(CHUNKS)]
    + [f"gf{k}_{i}" for k in range(4) for i in range(CHUNKS)]
    + ["we", "wp", "wq"]
    + [f"w{s}x{k}" for s in "epq" for k in range(3)]
    + [f"w{s}f{k}" for s in "epq" for k in range(4)]
    + [f"d{k}_{g}" for k in range(3) for g in range(2)]
    + ["ml0", "ml1"]
    + ["gain0", "gain1"]
)
SEM = {name: i for i, name in enumerate(NAMES)}


def body(
    frames, lengths, ln_gain, ln_bias, glu_w, taps_in, bn_gain, bn_bias, out_w, out,
    xin, lng, lnb, tin, bg, bb, own, nbuf, wg, wf, pack, par, gs, cv, dsend, dbuf,
    msg, plane, bmsg, gmsg, ball, gall, mlx, act,
    lsem, ssem, rsem, asend, arecv, bsend, brecv,
):
    dp = lax.axis_index("dp")
    t = lax.axis_index("tensor")
    x, yh, z = dp // 16, (dp // 8) % 2, dp % 8
    y, c = t // 2, t % 2
    h, j = y // 2, y % 2
    me = yh * 8 + t
    sib = t + 1 - 2 * c
    par_t = (y + 1 - 2 * j) * 2 + c
    ext_t = (3 - y) * 2 + c
    ext_s = (3 - y) * 2 + 1 - c
    edge = (y == 0) | (y == 3)
    ext_dp = jnp.where(edge, dp + 8 - 16 * yh, dp)
    pe_t = (3 - (y + 1 - 2 * j)) * 2 + c

    colour = (x + 2 * z) % 4
    near = [
        ((((x + 1) % 4) * 2 + yh) * 8 + z, (colour + 1) % 4, 1),
        ((((x + 3) % 4) * 2 + yh) * 8 + z, (colour + 3) % 4, 0),
        ((x * 2 + yh) * 8 + z + 1 - 2 * (z % 2), (colour + 2) % 4, 2),
    ]
    sent = []

    def send(src, dst, recv, tensor, to_dp=dp, cond=None):
        copy = pltpu.make_async_remote_copy(
            src_ref=src, dst_ref=dst, send_sem=ssem.at[len(sent)], recv_sem=rsem.at[SEM[recv]],
            device_id={"dp": to_dp, "tensor": tensor}, device_id_type=MESH,
        )
        sent.append((cond, copy))
        if cond is None:
            copy.start()
        else:
            pl.when(cond)(copy.start)

    def arrived(dst, recv):
        pltpu.make_async_remote_copy(
            src_ref=dst, dst_ref=dst, send_sem=ssem.at[0], recv_sem=rsem.at[SEM[recv]],
            device_id={"dp": dp, "tensor": sib}, device_id_type=MESH,
        ).wait_recv()

    barrier = pltpu.get_barrier_semaphore()

    def greet_plane(i, _):
        to = (((x + i // 8) % 4) * 2 + yh) * 8 + (z + i % 8) % 8
        pl.semaphore_signal(barrier, inc=1, device_id={"dp": to, "tensor": t}, device_id_type=MESH)
        return 0

    def greet_line(i, _):
        q = (me + i) % 16
        to = (x * 2 + q // 8) * 8 + z
        pl.semaphore_signal(barrier, inc=1, device_id={"dp": to, "tensor": q % 8}, device_id_type=MESH)
        return 0

    lax.fori_loop(1, 16, greet_line, 0)
    lax.fori_loop(1, 32, greet_plane, 0)

    loads = [
        pltpu.make_async_copy(frames.at[0], xin, lsem.at[0]),
        pltpu.make_async_copy(ln_gain, lng, lsem.at[1]),
        pltpu.make_async_copy(ln_bias, lnb, lsem.at[2]),
        pltpu.make_async_copy(taps_in, tin, lsem.at[3]),
        pltpu.make_async_copy(bn_gain, bg, lsem.at[4]),
        pltpu.make_async_copy(bn_bias, bb, lsem.at[5]),
        pltpu.make_async_copy(glu_w, wg.at[h, :, pl.ds(pl.multiple_of(SHARD * c, 64), SHARD)], lsem.at[6]),
        pltpu.make_async_copy(out_w, wf.at[pl.ds(pl.multiple_of(SHARD * t, 64), SHARD)], lsem.at[7]),
    ]
    for copy in loads:
        copy.start()
    for copy in loads[:6]:
        copy.wait()

    rows = xin[...].astype(F32)
    center = jnp.mean(rows, axis=-1, keepdims=True)
    spread = jnp.mean((rows - center) ** 2, axis=-1, keepdims=True)
    own[...] = ((rows - center) * lax.rsqrt(spread + 1e-05) * lng[...][None, :] + lnb[...][None, :]).astype(BF16)

    pack[0] = jnp.zeros_like(pack[0])
    pack[0, 0:TAPS, 0:SHARD] = tin[...].astype(F32)
    pack[0, TAPS : TAPS + 1, 0:SHARD] = bg[...][None, :]
    pack[0, TAPS + 1 : TAPS + 2, 0:SHARD] = bb[...][None, :]

    same = (y + 2 * c - 1) // 2 == h
    gives = ((c == 1) & (y < 3)) | ((c == 0) & (y > 0))
    y2 = y + 2 * c - 1
    h2, j2 = y2 // 2, (y2 + 2) % 2
    mine = j == c

    @pl.when(mine)
    def _():
        nbuf[pl.ds(pl.multiple_of(HALO + ROWS * c, 16), ROWS), :] = own[...]

    @pl.when((c == 1) & (j == 0))
    def _():
        nbuf[0:HALO, :] = own[ROWS - HALO : ROWS, :]

    @pl.when((c == 0) & (j == 1))
    def _():
        nbuf[WIN - HALO : WIN, :] = own[0:HALO, :]

    @pl.when((c == 0) & (h == 0))
    def _():
        nbuf[0:HALO, :] = jnp.zeros((HALO, D), BF16)

    @pl.when((c == 1) & (h == 1))
    def _():
        nbuf[WIN - HALO : WIN, :] = jnp.zeros((HALO, D), BF16)

    pl.semaphore_wait(barrier, 46)

    def glu_rows(slot, core, quarter, i):
        first = SHARD * core + QUARTER * quarter + CROWS * i
        return wg.at[slot, :, pl.ds(pl.multiple_of(first, 16), CROWS)]

    for i in range(CHUNKS):
        src = glu_w.at[:, pl.ds(pl.multiple_of(QUARTER * colour + CROWS * i, 16), CROWS)]
        send(src, glu_rows(h, c, colour, i), f"gy{i}", ext_t, ext_dp)

    away = jnp.logical_not(mine)
    spot = nbuf.at[pl.ds(pl.multiple_of(HALO + ROWS * c, 16), ROWS)]
    for core in range(2):
        send(own, spot, f"blk{core}", (y + 1 - 2 * j) * 2 + j, cond=c == core)
        send(own, spot, f"blk{core}", sib, cond=(c == core) & away)

    low = nbuf.at[0:HALO]
    high = nbuf.at[WIN - HALO : WIN]
    tail = own.at[ROWS - HALO : ROWS]
    head = own.at[0:HALO]
    halo_a = jnp.where(same, par_t, (2 * h2) * 2 + j2)
    halo_b = (2 * h2 + 1) * 2 + j2
    apart = jnp.logical_not(same)
    send(tail, low, "low", halo_a, cond=(c == 1) & gives)
    send(tail, low, "low", halo_b, cond=(c == 1) & gives & apart)
    send(head, high, "high", halo_a, cond=(c == 0) & gives)
    send(head, high, "high", halo_b, cond=(c == 0) & gives & apart)

    send(glu_w, wg.at[h, :, pl.ds(pl.multiple_of(SHARD * c, 64), SHARD)], "glu_sib", sib)
    send(pack.at[0], pack.at[1], "pack_s", sib)
    send(pack.at[0], pack.at[2], "pack_e", ext_t, ext_dp)
    send(pack.at[0], pack.at[3], "pack_d", ext_s, ext_dp)

    def w_rows(shard, first=0, n=SHARD):
        return wf.at[pl.ds(pl.multiple_of(SHARD * shard + first, 16), n)]

    def w_quarter(shard, quarter):
        return w_rows(shard, QUARTER * quarter, QUARTER)

    send(out_w, w_rows(t), "w_sib", sib)

    lane = lax.broadcasted_iota(jnp.int32, (40, 128), 1)

    def tiles_of(slot, mine_at, other_at):
        a = pack[mine_at]
        b = pack[other_at]
        first = jnp.where(c == 0, a, b)
        second = jnp.where(c == 0, b, a)
        r0 = pltpu.roll(second[:, 0:128], 64, 1)
        r1 = pltpu.roll(second[:, 128:256], 64, 1)
        par[3 * slot] = first[:, 0:128]
        par[3 * slot + 1] = jnp.where(lane < 64, first[:, 128:256], r0)
        par[3 * slot + 2] = jnp.where(lane < 64, r0, r1)

    arrived(pack.at[1], "pack_s")
    tiles_of(h, 0, 1)
    arrived(pack.at[2], "pack_e")
    arrived(pack.at[3], "pack_d")
    tiles_of(1 - h, 2, 3)
    gmsg[...] = jnp.zeros_like(gmsg)
    for k in range(6):
        gmsg[k : k + 1, :] = par[k, TAPS : TAPS + 1, :]
        gmsg[8 + k : 9 + k, :] = par[k, TAPS + 1 : TAPS + 2, :]

    for giver in range(2):
        is_giver = t == 2 * giver
        for i in range(1, 8):
            send(gmsg, gall.at[giver], f"gain{giver}", (t + i) % 8, cond=is_giver)

        @pl.when(is_giver)
        def _(giver=giver):
            gall[giver] = gmsg[...]

    length = lengths[0]
    start = 2 * SPAN * h + SPAN * c
    count = jnp.clip(length - start, 0, SPAN)
    count_f = count.astype(F32)
    inverse = 1.0 / jnp.maximum(count_f, 1.0)
    msg[...] = jnp.zeros_like(msg)
    msg[6:7, :] = jnp.full((1, 128), count_f, F32)

    def one_tile(slot, q):
        k = 3 * slot + q
        w = wg[slot, :, pl.ds(pl.multiple_of(128 * q, 128), 128), :].reshape(256, D)
        both = lax.dot_general(nbuf[...], w, (((1,), (1,)), ((), ())), preferred_element_type=F32)
        glu = (both[:, 0:128] * jax.nn.sigmoid(both[:, 128:256])).astype(BF16).astype(F32)
        at = lax.broadcasted_iota(jnp.int32, (WIN, 128), 0)
        gs[...] = jnp.where(at < length - start + HALO, glu, 0.0)
        step = 64

        def conv_rows(i, total):
            first = pl.multiple_of(i * step, step)
            acc = jnp.zeros((step, 128), F32)
            for tap in range(TAPS):
                acc = acc + gs[pl.ds(first + (tap + 1), step), :] * par[k, tap : tap + 1, :]
            cv[pl.ds(first, step), :] = acc
            here = first + lax.broadcasted_iota(jnp.int32, (step, 128), 0)
            kept = jnp.where(here < count, acc, 0.0)
            return total + jnp.sum(kept.reshape(step // 8, 8, 128), axis=0)

        total = lax.fori_loop(0, SPAN // step, conv_rows, jnp.zeros((8, 128), F32))
        local = jnp.sum(total, axis=0, keepdims=True) * inverse
        dev = cv[...] - local
        dsend[k] = dev.astype(BF16)
        here = lax.broadcasted_iota(jnp.int32, (SPAN, 128), 0)
        kept = jnp.where(here < count, dev, 0.0)
        msg[pl.ds(k, 1), :] = local
        msg[pl.ds(8 + k, 1), :] = jnp.sum(kept * kept, axis=0, keepdims=True)

    owner = 2 * (2 * h + c)
    shard_of = (jnp.minimum(y, 3 - y), jnp.maximum(y, 3 - y))

    def give(slot, q, n, group):
        base = 3 * jnp.where(slot == 0, shard_of[0], shard_of[1]) + q
        for g in range(2):
            src = dsend.at[pl.ds(3 * slot + q, n), pl.ds(ROWS * g, ROWS)]
            dst = dbuf.at[pl.ds(base, n)]
            kept = mine & (c == g)
            for s in range(2):
                send(src, dst, f"d{group}_{s}", owner + g, cond=jnp.logical_not(kept) & (j == s))

            @pl.when(kept)
            def _(src=src, dst=dst):
                keep = pltpu.make_async_copy(src, dst, lsem.at[8])
                keep.start()
                keep.wait()

    for i in range(CHUNKS):
        at = glu_rows(1 - h, c, colour, i)
        arrived(at, f"gy{i}")
        for to_dp, _, k in near:
            send(at, at, f"gx{k}_{i}", t, to_dp)
        send(at, at, f"gf3_{i}", sib)

    def pass_glu(i):
        for k, (_, their, _) in enumerate(near):
            at = glu_rows(1 - h, c, their, i)
            arrived(at, f"gx{k}_{i}")
            send(at, at, f"gf{k}_{i}", sib)

    for p in range(2):
        @pl.when(jnp.logical_not(mine & (c == p)))
        def _(p=p):
            arrived(nbuf.at[HALO + ROWS * p : HALO + ROWS * (p + 1)], f"blk{p}")

    @pl.when(((c == 1) & (j == 1)) | ((c == 0) & (h == 1)))
    def _():
        arrived(low, "low")

    @pl.when(((c == 0) & (j == 0)) | ((c == 1) & (h == 0)))
    def _():
        arrived(high, "high")

    loads[6].wait()
    arrived(wg.at[h, :, pl.ds(pl.multiple_of(SHARD * (1 - c), 64), SHARD)], "glu_sib")

    w_mine = out_w.at[pl.ds(pl.multiple_of(QUARTER * colour, 16), QUARTER)]
    send(w_mine, w_quarter(t, colour), "we", ext_t, ext_dp)
    send(w_mine, w_quarter(t, colour), "wp", par_t)

    one_tile(h, 0)
    pass_glu(0)
    one_tile(h, 1)
    pass_glu(1)
    one_tile(h, 2)
    pass_glu(2)
    give(h, 0, 3, 0)

    w_from = {"e": ext_t, "p": par_t, "q": pe_t}

    def w_on(s):
        at = w_quarter(w_from[s], colour)
        arrived(at, f"w{s}")
        if s == "e":
            send(at, at, "wq", par_t)
        for to_dp, _, k in near:
            send(at, at, f"w{s}x{k}", t, to_dp)
        send(at, at, f"w{s}f3", sib)

    def w_last(s):
        for k, (_, their, _) in enumerate(near):
            at = w_quarter(w_from[s], their)
            arrived(at, f"w{s}x{k}")
            send(at, at, f"w{s}f{k}", sib)

    quarters = [their for _, their, _ in near] + [colour]
    for i in range(CHUNKS):
        for k in range(4):
            arrived(glu_rows(1 - h, 1 - c, quarters[k], i), f"gf{k}_{i}")
    one_tile(1 - h, 0)
    w_on("e")
    w_on("p")
    one_tile(1 - h, 1)
    give(1 - h, 0, 1, 1)
    one_tile(1 - h, 2)

    def plane_copy(i):
        to = (((x + i // 8) % 4) * 2 + yh) * 8 + (z + i % 8) % 8
        return pltpu.make_async_remote_copy(
            src_ref=msg, dst_ref=plane.at[i], send_sem=asend.at[i], recv_sem=arecv.at[i],
            device_id={"dp": to, "tensor": t}, device_id_type=MESH,
        )

    def send_plane(i, _):
        plane_copy(i).start()
        return 0

    lax.fori_loop(1, 32, send_plane, 0)
    give(1 - h, 1, 2, 2)
    u = jnp.where(edge, 0, 1)
    for g in range(2):
        for s in range(2):
            send(msg.at[0:8], mlx.at[s], f"ml{s}", owner + g, cond=jnp.logical_not(mine & (c == g)) & (u == s))

    @pl.when(mine)
    def _():
        mlx[u] = msg[0:8, :]

    w_on("q")

    def merge(blocks):
        n = sum(jnp.broadcast_to(b[6:7, :], (8, 128)) for b in blocks)
        weighted = sum(jnp.broadcast_to(b[6:7, :], (8, 128)) * b[0:8, :] for b in blocks)
        mean = weighted / jnp.maximum(n, 1.0)
        square = sum(
            b[8:16, :] + jnp.broadcast_to(b[6:7, :], (8, 128)) * (b[0:8, :] - mean) ** 2 for b in blocks
        )
        return n, mean, square

    def wait_plane(i, _):
        plane_copy(i).wait_recv()
        return 0

    lax.fori_loop(1, 32, wait_plane, 0)
    plane[0] = msg[...]
    n, mean, square = merge([plane[i] for i in range(32)])
    row = lax.broadcasted_iota(jnp.int32, (8, 128), 0)
    bmsg[0:8, :] = jnp.where(row == 6, n, mean)
    bmsg[8:16, :] = square

    def line(i, src, dst, ss, rs):
        q = (me + i) % 16
        to = (x * 2 + q // 8) * 8 + z
        return pltpu.make_async_remote_copy(
            src_ref=src, dst_ref=dst.at[me], send_sem=ss.at[i], recv_sem=rs.at[me],
            device_id={"dp": to, "tensor": q % 8}, device_id_type=MESH,
        )

    def send_line(i, _):
        line(i, bmsg, ball, bsend, brecv).start()
        return 0

    lax.fori_loop(1, 16, send_line, 0)
    ball[me] = bmsg[...]

    for s in "epq":
        w_last(s)

    def wait_line(i, _):
        q = (me + i) % 16
        pltpu.make_async_remote_copy(
            src_ref=bmsg, dst_ref=ball.at[q], send_sem=bsend.at[0], recv_sem=brecv.at[q],
            device_id={"dp": dp, "tensor": sib}, device_id_type=MESH,
        ).wait_recv()
        return 0

    lax.fori_loop(1, 16, wait_line, 0)

    for group, n in ((0, 3), (1, 1), (2, 2)):
        for s in range(2):
            @pl.when(jnp.logical_not((j == s) & mine))
            def _(group=group, n=n, s=s):
                arrived(dbuf.at[pl.ds(0, n)], f"d{group}_{s}")
    for s in range(2):
        @pl.when(jnp.logical_not((u == s) & mine))
        def _(s=s):
            arrived(mlx.at[s], f"ml{s}")

    for giver in range(2):
        @pl.when(t != 2 * giver)
        def _(giver=giver):
            arrived(gall.at[giver], f"gain{giver}")

    sets = ((0, 1, 6, 7), (2, 3, 4, 5))
    offset, scale, shift = [], [], []
    for s in range(2):
        n, mean, square = merge([ball[8 * g + q] for g in range(2) for q in sets[s]])
        n1 = jnp.broadcast_to(n[0:1, :], (8, 128))
        gains = gall[s]
        offset.append(mlx[s] - mean)
        scale.append(lax.rsqrt(square / n1 + 1e-05) * gains[0:8, :])
        shift.append(gains[8:16, :])
    where = [(0, 0), (0, 1), (0, 2), (1, 0), (1, 1), (1, 2), (1, 3), (1, 4), (1, 5), (0, 3), (0, 4), (0, 5)]
    for g, (s, r) in enumerate(where):
        zed = (dbuf[g].astype(F32) + offset[s][r : r + 1, :]) * scale[s][r : r + 1, :] + shift[s][r : r + 1, :]
        act[:, 128 * g : 128 * (g + 1)] = (zed * jax.nn.sigmoid(zed)).astype(BF16)

    loads[7].wait()
    arrived(w_rows(sib), "w_sib")
    for s in "epq":
        for k in range(4):
            arrived(w_quarter(w_from[s] + 1 - 2 * c, quarters[k]), f"w{s}f{k}")

    def columns(i, _):
        at = pl.multiple_of(256 * i, 256)
        branch = lax.dot_general(
            act[...], wf[pl.ds(at, 256), :], (((1,), (1,)), ((), ())), preferred_element_type=F32
        )
        out[0, :, pl.ds(at, 256)] = (xin[:, pl.ds(at, 256)].astype(F32) + branch).astype(BF16)
        return 0

    lax.fori_loop(0, D // 256, columns, 0)

    for cond, copy in sent:
        if cond is None:
            copy.wait_send()
        else:
            pl.when(cond)(copy.wait_send)

    def sent_plane(i, _):
        plane_copy(i).wait_send()
        return 0

    def sent_line(i, _):
        line(i, bmsg, ball, bsend, brecv).wait_send()
        return 0

    lax.fori_loop(1, 32, sent_plane, 0)
    lax.fori_loop(1, 16, sent_line, 0)


def per_device(
    frames_in, lengths, ln_gain, ln_bias, glu_weight, conv_kernel, bn_gain, bn_bias, out_weight
):
    hbm = pl.BlockSpec(memory_space=pltpu.HBM)
    dma = pltpu.SemaphoreType.DMA
    return pl.pallas_call(
        body,
        out_shape=jax.ShapeDtypeStruct((1, ROWS, D), BF16),
        in_specs=[hbm, pl.BlockSpec(memory_space=pltpu.SMEM)] + [hbm] * 7,
        out_specs=pl.BlockSpec(memory_space=pltpu.VMEM),
        scratch_shapes=[
            pltpu.VMEM((ROWS, D), BF16),
            pltpu.VMEM((D,), F32),
            pltpu.VMEM((D,), F32),
            pltpu.VMEM((TAPS, SHARD), BF16),
            pltpu.VMEM((SHARD,), F32),
            pltpu.VMEM((SHARD,), F32),
            pltpu.VMEM((ROWS, D), BF16),
            pltpu.VMEM((WIN, D), BF16),
            pltpu.VMEM((2, 2, CHIP, D), BF16),
            pltpu.VMEM((D, D), BF16),
            pltpu.VMEM((4, 40, 256), F32),
            pltpu.VMEM((6, 40, 128), F32),
            pltpu.VMEM((WIN, 128), F32),
            pltpu.VMEM((SPAN, 128), F32),
            pltpu.VMEM((6, SPAN, 128), BF16),
            pltpu.VMEM((12, ROWS, 128), BF16),
            pltpu.VMEM((16, 128), F32),
            pltpu.VMEM((32, 16, 128), F32),
            pltpu.VMEM((16, 128), F32),
            pltpu.VMEM((16, 128), F32),
            pltpu.VMEM((16, 16, 128), F32),
            pltpu.VMEM((2, 16, 128), F32),
            pltpu.VMEM((2, 8, 128), F32),
            pltpu.VMEM((ROWS, D), BF16),
            dma((9,)),
            dma((SENDS,)),
            dma((len(NAMES),)),
            dma((32,)),
            dma((32,)),
            dma((16,)),
            dma((16,)),
        ],
        compiler_params=pltpu.CompilerParams(
            collective_id=0, has_side_effects=True, vmem_limit_bytes=(64 << 20) - (128 << 10)
        ),
    )(
        frames_in, lengths, ln_gain, ln_bias, glu_weight, conv_kernel,
        bn_gain, bn_bias, out_weight,
    )


def solution(mesh):
    return jax.shard_map(
        per_device,
        mesh=mesh,
        in_specs=(
            P("dp", "tensor", None),
            P("dp"),
            P(),
            P(),
            P(None, "tensor", None),
            P(None, "tensor"),
            P("tensor"),
            P("tensor"),
            P("tensor", None),
        ),
        out_specs=P("dp", "tensor", None),
        check_vma=False,
    )
```

```python
import functools

import jax
import jax.numpy as jnp
from jax import lax
from jax.experimental import pallas as pl
from jax.experimental.pallas import tpu as pltpu
from jax.sharding import PartitionSpec as P

MESH = pl.DeviceIdType.MESH
F32 = jnp.float32
BF16 = jnp.bfloat16
TAPS = 32
D = 1536
SHARD = 192
CHIP = 384
ROWS = 128
HALO = 16
SPAN = 2 * ROWS
WIN = SPAN + 2 * HALO
QUARTER = SHARD // 4
CHUNKS = 3
CROWS = QUARTER // CHUNKS
LNS = 4
LROWS = ROWS // LNS
SENDS = 160

NAMES = (
    ["glu_sib", "low", "high", "pack_s", "pack_e", "pack_d", "w_sib"]
    + [f"blk{p}_{i}" for p in range(2) for i in range(LNS)]
    + [f"gy{i}" for i in range(CHUNKS)]
    + [f"gx{k}_{i}" for k in range(3) for i in range(CHUNKS)]
    + [f"gf{k}_{i}" for k in range(4) for i in range(CHUNKS)]
    + ["we", "wp", "wq"]
    + [f"w{s}x{k}" for s in "epq" for k in range(3)]
    + [f"w{s}f{k}" for s in "epq" for k in range(4)]
    + [f"d{k}_{g}" for k in range(3) for g in range(2)]
    + ["ml0", "ml1"]
    + ["gain0", "gain1"]
)
SEM = {name: i for i, name in enumerate(NAMES)}


def body(
    frames, lengths, ln_gain, ln_bias, glu_w, taps_in, bn_gain, bn_bias, out_w, out,
    xin, lng, lnb, tin, bg, bb, own, nbuf, wg, wf, pack, par, gs, cv, dsend, dbuf,
    msg, plane, bmsg, gmsg, ball, gall, mlx, mlm, act,
    lsem, ssem, rsem, asend, arecv, bsend, brecv,
):
    dp = lax.axis_index("dp")
    t = lax.axis_index("tensor")
    x, yh, z = dp // 16, (dp // 8) % 2, dp % 8
    y, c = t // 2, t % 2
    h, j = y // 2, y % 2
    me = yh * 8 + t
    sib = t + 1 - 2 * c
    par_t = (y + 1 - 2 * j) * 2 + c
    ext_t = (3 - y) * 2 + c
    ext_s = (3 - y) * 2 + 1 - c
    edge = (y == 0) | (y == 3)
    ext_dp = jnp.where(edge, dp + 8 - 16 * yh, dp)
    pe_t = (3 - (y + 1 - 2 * j)) * 2 + c

    colour = (x + 2 * z) % 4
    near = [
        ((((x + 1) % 4) * 2 + yh) * 8 + z, (colour + 1) % 4, 1),
        ((((x + 3) % 4) * 2 + yh) * 8 + z, (colour + 3) % 4, 0),
        ((x * 2 + yh) * 8 + z + 1 - 2 * (z % 2), (colour + 2) % 4, 2),
    ]
    sent = []

    def send(src, dst, recv, tensor, to_dp=dp, cond=None):
        copy = pltpu.make_async_remote_copy(
            src_ref=src, dst_ref=dst, send_sem=ssem.at[len(sent)], recv_sem=rsem.at[SEM[recv]],
            device_id={"dp": to_dp, "tensor": tensor}, device_id_type=MESH,
        )
        sent.append((cond, copy))
        if cond is None:
            copy.start()
        else:
            pl.when(cond)(copy.start)

    def arrived(dst, recv):
        pltpu.make_async_remote_copy(
            src_ref=dst, dst_ref=dst, send_sem=ssem.at[0], recv_sem=rsem.at[SEM[recv]],
            device_id={"dp": dp, "tensor": sib}, device_id_type=MESH,
        ).wait_recv()

    barrier = pltpu.get_barrier_semaphore()

    loads = [
        pltpu.make_async_copy(frames.at[0], xin, lsem.at[0]),
        pltpu.make_async_copy(ln_gain, lng, lsem.at[1]),
        pltpu.make_async_copy(ln_bias, lnb, lsem.at[2]),
        pltpu.make_async_copy(taps_in, tin, lsem.at[3]),
        pltpu.make_async_copy(bn_gain, bg, lsem.at[4]),
        pltpu.make_async_copy(bn_bias, bb, lsem.at[5]),
        pltpu.make_async_copy(glu_w, wg.at[h, :, pl.ds(pl.multiple_of(SHARD * c, 64), SHARD)], lsem.at[6]),
        pltpu.make_async_copy(out_w, wf.at[pl.ds(pl.multiple_of(SHARD * t, 64), SHARD)], lsem.at[7]),
    ]
    for copy in loads:
        copy.start()

    def greet_plane(i, _):
        to = (((x + i // 8) % 4) * 2 + yh) * 8 + (z + i % 8) % 8
        pl.semaphore_signal(barrier, inc=1, device_id={"dp": to, "tensor": t}, device_id_type=MESH)
        return 0

    def greet_line(i, _):
        q = (me + i) % 16
        to = (x * 2 + q // 8) * 8 + z
        pl.semaphore_signal(barrier, inc=1, device_id={"dp": to, "tensor": q % 8}, device_id_type=MESH)
        return 0

    lax.fori_loop(1, 16, greet_line, 0)
    lax.fori_loop(1, 32, greet_plane, 0)

    pl.semaphore_wait(barrier, 46)

    same = (y + 2 * c - 1) // 2 == h
    gives = ((c == 1) & (y < 3)) | ((c == 0) & (y > 0))
    y2 = y + 2 * c - 1
    h2, j2 = y2 // 2, (y2 + 2) % 2
    mine = j == c

    def glu_rows(slot, core, quarter, i):
        first = SHARD * core + QUARTER * quarter + CROWS * i
        return wg.at[slot, :, pl.ds(pl.multiple_of(first, 16), CROWS)]

    def w_rows(shard, first=0, n=SHARD):
        return wf.at[pl.ds(pl.multiple_of(SHARD * shard + first, 16), n)]

    def w_quarter(shard, quarter):
        return w_rows(shard, QUARTER * quarter, QUARTER)

    for i in range(CHUNKS):
        src = glu_w.at[:, pl.ds(pl.multiple_of(QUARTER * colour + CROWS * i, 16), CROWS)]
        send(src, glu_rows(h, c, colour, i), f"gy{i}", ext_t, ext_dp)
    send(glu_w, wg.at[h, :, pl.ds(pl.multiple_of(SHARD * c, 64), SHARD)], "glu_sib", sib)

    for copy in loads[:3]:
        copy.wait()
    away = jnp.logical_not(mine)
    for i in range(LNS):
        at = slice(LROWS * i, LROWS * (i + 1))
        rows = xin[at, :].astype(F32)
        center = jnp.mean(rows, axis=-1, keepdims=True)
        spread = jnp.mean((rows - center) ** 2, axis=-1, keepdims=True)
        own[at, :] = (
            (rows - center) * lax.rsqrt(spread + 1e-05) * lng[...][None, :] + lnb[...][None, :]
        ).astype(BF16)
        spot = nbuf.at[pl.ds(pl.multiple_of(HALO + ROWS * c + LROWS * i, 16), LROWS)]
        for core in range(2):
            send(own.at[at], spot, f"blk{core}_{i}", (y + 1 - 2 * j) * 2 + j, cond=c == core)
            send(own.at[at], spot, f"blk{core}_{i}", sib, cond=(c == core) & away)

    low = nbuf.at[0:HALO]
    high = nbuf.at[WIN - HALO : WIN]
    tail = own.at[ROWS - HALO : ROWS]
    head = own.at[0:HALO]
    halo_a = jnp.where(same, par_t, (2 * h2) * 2 + j2)
    halo_b = (2 * h2 + 1) * 2 + j2
    apart = jnp.logical_not(same)
    send(tail, low, "low", halo_a, cond=(c == 1) & gives)
    send(tail, low, "low", halo_b, cond=(c == 1) & gives & apart)
    send(head, high, "high", halo_a, cond=(c == 0) & gives)
    send(head, high, "high", halo_b, cond=(c == 0) & gives & apart)

    for copy in loads[3:6]:
        copy.wait()
    pack[0] = jnp.zeros_like(pack[0])
    pack[0, 0:TAPS, 0:SHARD] = tin[...].astype(F32)
    pack[0, TAPS : TAPS + 1, 0:SHARD] = bg[...][None, :]
    pack[0, TAPS + 1 : TAPS + 2, 0:SHARD] = bb[...][None, :]
    send(pack.at[0], pack.at[1], "pack_s", sib)
    send(pack.at[0], pack.at[2], "pack_e", ext_t, ext_dp)

    @pl.when(mine)
    def _():
        nbuf[pl.ds(pl.multiple_of(HALO + ROWS * c, 16), ROWS), :] = own[...]

    @pl.when((c == 1) & (j == 0))
    def _():
        nbuf[0:HALO, :] = own[ROWS - HALO : ROWS, :]

    @pl.when((c == 0) & (j == 1))
    def _():
        nbuf[WIN - HALO : WIN, :] = own[0:HALO, :]

    @pl.when((c == 0) & (h == 0))
    def _():
        nbuf[0:HALO, :] = jnp.zeros((HALO, D), BF16)

    @pl.when((c == 1) & (h == 1))
    def _():
        nbuf[WIN - HALO : WIN, :] = jnp.zeros((HALO, D), BF16)

    lane = lax.broadcasted_iota(jnp.int32, (40, 128), 1)

    def tiles_of(slot, mine_at, other_at):
        a = pack[mine_at]
        b = pack[other_at]
        first = jnp.where(c == 0, a, b)
        second = jnp.where(c == 0, b, a)
        r0 = pltpu.roll(second[:, 0:128], 64, 1)
        r1 = pltpu.roll(second[:, 128:256], 64, 1)
        par[3 * slot] = first[:, 0:128]
        par[3 * slot + 1] = jnp.where(lane < 64, first[:, 128:256], r0)
        par[3 * slot + 2] = jnp.where(lane < 64, r0, r1)

    arrived(pack.at[1], "pack_s")
    tiles_of(h, 0, 1)
    length = lengths[0]
    start = 2 * SPAN * h + SPAN * c
    count = jnp.clip(length - start, 0, SPAN)
    count_f = count.astype(F32)
    inverse = 1.0 / jnp.maximum(count_f, 1.0)
    msg[...] = jnp.zeros_like(msg)
    mlm[...] = jnp.zeros_like(mlm)
    for kind in range(2):
        msg[kind, 6:7, :] = jnp.full((1, 128), count_f, F32)

    def one_tile(slot, q, kind):
        k = 3 * slot + q
        w = wg[slot, :, pl.ds(pl.multiple_of(128 * q, 128), 128), :].reshape(256, D)
        both = lax.dot_general(nbuf[...], w, (((1,), (1,)), ((), ())), preferred_element_type=F32)
        glu = (both[:, 0:128] * jax.nn.sigmoid(both[:, 128:256])).astype(BF16).astype(F32)
        at = lax.broadcasted_iota(jnp.int32, (WIN, 128), 0)
        gs[...] = jnp.where(at < length - start + HALO, glu, 0.0)
        step = 64

        def conv_rows(i, total):
            first = pl.multiple_of(i * step, step)
            acc = jnp.zeros((step, 128), F32)
            for tap in range(TAPS):
                acc = acc + gs[pl.ds(first + (tap + 1), step), :] * par[k, tap : tap + 1, :]
            cv[pl.ds(first, step), :] = acc
            here = first + lax.broadcasted_iota(jnp.int32, (step, 128), 0)
            kept = jnp.where(here < count, acc, 0.0)
            return total + jnp.sum(kept.reshape(step // 8, 8, 128), axis=0)

        total = lax.fori_loop(0, SPAN // step, conv_rows, jnp.zeros((8, 128), F32))
        local = jnp.sum(total, axis=0, keepdims=True) * inverse
        dev = cv[...] - local
        dsend[k] = dev.astype(BF16)
        here = lax.broadcasted_iota(jnp.int32, (SPAN, 128), 0)
        kept = jnp.where(here < count, dev, 0.0)
        mlm[pl.ds(k, 1), :] = local
        msg[kind, q : q + 1, :] = local
        msg[kind, 3 + q : 4 + q, :] = jnp.sum(kept * kept, axis=0, keepdims=True)

    owner = 2 * (2 * h + c)
    shard_of = (jnp.minimum(y, 3 - y), jnp.maximum(y, 3 - y))

    def give(slot, q, n, group):
        base = 3 * jnp.where(slot == 0, shard_of[0], shard_of[1]) + q
        for g in range(2):
            src = dsend.at[pl.ds(3 * slot + q, n), pl.ds(ROWS * g, ROWS)]
            dst = dbuf.at[pl.ds(base, n)]
            kept = mine & (c == g)
            for s in range(2):
                send(src, dst, f"d{group}_{s}", owner + g, cond=jnp.logical_not(kept) & (j == s))

            @pl.when(kept)
            def _(src=src, dst=dst):
                keep = pltpu.make_async_copy(src, dst, lsem.at[8])
                keep.start()
                keep.wait()

    w_mine = out_w.at[pl.ds(pl.multiple_of(QUARTER * colour, 16), QUARTER)]
    for i in range(CHUNKS):
        at = glu_rows(1 - h, c, colour, i)
        arrived(at, f"gy{i}")
        for to_dp, _, k in near:
            send(at, at, f"gx{k}_{i}", t, to_dp)
        send(at, at, f"gf3_{i}", sib)
        if i == 1:
            send(w_mine, w_quarter(t, colour), "we", ext_t, ext_dp)

    def pass_glu(i):
        for k, (_, their, _) in enumerate(near):
            at = glu_rows(1 - h, c, their, i)
            arrived(at, f"gx{k}_{i}")
            send(at, at, f"gf{k}_{i}", sib)

    def plane_copy(i, kind):
        to = (((x + i // 8) % 4) * 2 + yh) * 8 + (z + i % 8) % 8
        return pltpu.make_async_remote_copy(
            src_ref=msg.at[kind], dst_ref=plane.at[kind, i], send_sem=asend.at[kind, i], recv_sem=arecv.at[kind, i],
            device_id={"dp": to, "tensor": t}, device_id_type=MESH,
        )

    def line_copy(i, kind):
        q = (me + i) % 16
        to = (x * 2 + q // 8) * 8 + z
        return pltpu.make_async_remote_copy(
            src_ref=bmsg.at[kind], dst_ref=ball.at[kind, me], send_sem=bsend.at[kind, i], recv_sem=brecv.at[kind, me],
            device_id={"dp": to, "tensor": q % 8}, device_id_type=MESH,
        )

    def over(n, what):
        def step(i, _):
            what(i)
            return 0

        lax.fori_loop(1, n, step, 0)

    def merge(blocks):
        n = sum(jnp.broadcast_to(b[6:7, :], (8, 128)) for b in blocks)
        mean = sum(jnp.broadcast_to(b[6:7, :], (8, 128)) * b for b in blocks) / jnp.maximum(n, 1.0)
        apart = sum(jnp.broadcast_to(b[6:7, :], (8, 128)) * (b - mean) ** 2 for b in blocks)
        return n, mean, sum(blocks) + pltpu.roll(apart, 3, 0)

    row = lax.broadcasted_iota(jnp.int32, (8, 128), 0)

    def send_plane(kind):
        over(32, lambda i: plane_copy(i, kind).start())
        plane[kind, 0] = msg[kind]

    def plane_to_line(kind):
        over(32, lambda i: plane_copy(i, kind).wait_recv())
        n, mean, square = merge([plane[kind, i] for i in range(32)])
        bmsg[kind] = jnp.where(row < 3, mean, jnp.where(row == 6, n, square))
        over(16, lambda i: line_copy(i, kind).start())
        ball[kind, me] = bmsg[kind]

    for p in range(2):
        @pl.when(jnp.logical_not(mine & (c == p)))
        def _(p=p):
            for i in range(LNS):
                first = HALO + ROWS * p + LROWS * i
                arrived(nbuf.at[first : first + LROWS], f"blk{p}_{i}")

    @pl.when(((c == 1) & (j == 1)) | ((c == 0) & (h == 1)))
    def _():
        arrived(low, "low")

    @pl.when(((c == 0) & (j == 0)) | ((c == 1) & (h == 0)))
    def _():
        arrived(high, "high")

    loads[6].wait()
    arrived(wg.at[h, :, pl.ds(pl.multiple_of(SHARD * (1 - c), 64), SHARD)], "glu_sib")

    send(w_mine, w_quarter(t, colour), "wp", par_t)
    send(out_w, w_rows(t), "w_sib", sib)

    w_from = {"e": ext_t, "p": par_t, "q": pe_t}

    def w_on(s):
        at = w_quarter(w_from[s], colour)
        arrived(at, f"w{s}")
        if s == "e":
            send(at, at, "wq", par_t)
        for to_dp, _, k in near:
            send(at, at, f"w{s}x{k}", t, to_dp)
        send(at, at, f"w{s}f3", sib)

    def w_last(s):
        for k, (_, their, _) in enumerate(near):
            at = w_quarter(w_from[s], their)
            arrived(at, f"w{s}x{k}")
            send(at, at, f"w{s}f{k}", sib)

    one_tile(h, 0, 0)
    pass_glu(0)
    arrived(pack.at[2], "pack_e")
    send(pack.at[2], pack.at[3], "pack_d", sib)
    one_tile(h, 1, 0)
    pass_glu(1)
    w_on("e")
    one_tile(h, 2, 0)
    pass_glu(2)
    send_plane(0)
    give(h, 0, 3, 0)

    arrived(pack.at[3], "pack_d")
    tiles_of(1 - h, 2, 3)
    quarters = [their for _, their, _ in near] + [colour]
    for i in range(CHUNKS):
        for k in range(4):
            arrived(glu_rows(1 - h, 1 - c, quarters[k], i), f"gf{k}_{i}")
    one_tile(1 - h, 0, 1)
    one_tile(1 - h, 1, 1)
    give(1 - h, 0, 1, 1)
    one_tile(1 - h, 2, 1)
    send_plane(1)
    give(1 - h, 1, 2, 2)
    u = jnp.where(edge, 0, 1)
    for g in range(2):
        for s in range(2):
            send(mlm, mlx.at[s], f"ml{s}", owner + g, cond=jnp.logical_not(mine & (c == g)) & (u == s))

    @pl.when(mine)
    def _():
        mlx[u] = mlm[...]

    w_on("p")
    gmsg[...] = jnp.zeros_like(gmsg)
    for k in range(6):
        gmsg[k : k + 1, :] = par[k, TAPS : TAPS + 1, :]
        gmsg[8 + k : 9 + k, :] = par[k, TAPS + 1 : TAPS + 2, :]
    for giver in range(2):
        is_giver = t == 2 * giver
        for i in range(1, 8):
            send(gmsg, gall.at[giver], f"gain{giver}", (t + i) % 8, cond=is_giver)

        @pl.when(is_giver)
        def _(giver=giver):
            gall[giver] = gmsg[...]

    plane_to_line(0)
    w_on("q")
    w_last("e")
    plane_to_line(1)
    w_last("p")
    w_last("q")

    def line_arrived(i):
        q = (me + i) % 16
        for kind in range(2):
            pltpu.make_async_remote_copy(
                src_ref=bmsg.at[kind], dst_ref=ball.at[kind, q], send_sem=bsend.at[0, 0], recv_sem=brecv.at[kind, q],
                device_id={"dp": dp, "tensor": sib}, device_id_type=MESH,
            ).wait_recv()

    for group, n in ((0, 3), (1, 1), (2, 2)):
        for s in range(2):
            @pl.when(jnp.logical_not((j == s) & mine))
            def _(group=group, n=n, s=s):
                arrived(dbuf.at[pl.ds(0, n)], f"d{group}_{s}")
    for s in range(2):
        @pl.when(jnp.logical_not((u == s) & mine))
        def _(s=s):
            arrived(mlx.at[s], f"ml{s}")

    for giver in range(2):
        @pl.when(t != 2 * giver)
        def _(giver=giver):
            arrived(gall.at[giver], f"gain{giver}")

    over(16, line_arrived)
    for shard in range(4):
        from_own = [ball[0, 8 * g + 2 * shard + core] for g in range(2) for core in range(2)]
        from_extra = [ball[1, 8 * g + 2 * (3 - shard) + core] for g in range(2) for core in range(2)]
        n, mean, square = merge(from_own + from_extra)
        n1 = jnp.broadcast_to(n[0:1, :], (8, 128))
        pair = (0, 1, 1, 0)[shard]
        first = 3 * (shard // 2)
        root = lax.rsqrt(square / n1 + 1e-05)
        for r in range(3):
            g = 3 * shard + r
            k = first + r
            scale = root[3 + r : 4 + r, :] * gall[pair, k : k + 1, :]
            offset = mlx[pair, k : k + 1, :] - mean[r : r + 1, :]
            zed = (dbuf[g].astype(F32) + offset) * scale + gall[pair, 8 + k : 9 + k, :]
            act[:, 128 * g : 128 * (g + 1)] = (zed * jax.nn.sigmoid(zed)).astype(BF16)

    loads[7].wait()
    arrived(w_rows(sib), "w_sib")
    for s in "epq":
        for k in range(4):
            arrived(w_quarter(w_from[s] + 1 - 2 * c, quarters[k]), f"w{s}f{k}")

    def columns(i, _):
        at = pl.multiple_of(256 * i, 256)
        branch = lax.dot_general(
            act[...], wf[pl.ds(at, 256), :], (((1,), (1,)), ((), ())), preferred_element_type=F32
        )
        out[0, :, pl.ds(at, 256)] = (xin[:, pl.ds(at, 256)].astype(F32) + branch).astype(BF16)
        return 0

    lax.fori_loop(0, D // 256, columns, 0)

    for cond, copy in sent:
        if cond is None:
            copy.wait_send()
        else:
            pl.when(cond)(copy.wait_send)

    for kind in range(2):
        over(32, lambda i, kind=kind: plane_copy(i, kind).wait_send())
        over(16, lambda i, kind=kind: line_copy(i, kind).wait_send())


def per_device(
    frames_in, lengths, ln_gain, ln_bias, glu_weight, conv_kernel, bn_gain, bn_bias, out_weight
):
    hbm = pl.BlockSpec(memory_space=pltpu.HBM)
    dma = pltpu.SemaphoreType.DMA
    return pl.pallas_call(
        body,
        out_shape=jax.ShapeDtypeStruct((1, ROWS, D), BF16),
        in_specs=[hbm, pl.BlockSpec(memory_space=pltpu.SMEM)] + [hbm] * 7,
        out_specs=pl.BlockSpec(memory_space=pltpu.VMEM),
        scratch_shapes=[
            pltpu.VMEM((ROWS, D), BF16),
            pltpu.VMEM((D,), F32),
            pltpu.VMEM((D,), F32),
            pltpu.VMEM((TAPS, SHARD), BF16),
            pltpu.VMEM((SHARD,), F32),
            pltpu.VMEM((SHARD,), F32),
            pltpu.VMEM((ROWS, D), BF16),
            pltpu.VMEM((WIN, D), BF16),
            pltpu.VMEM((2, 2, CHIP, D), BF16),
            pltpu.VMEM((D, D), BF16),
            pltpu.VMEM((4, 40, 256), F32),
            pltpu.VMEM((6, 40, 128), F32),
            pltpu.VMEM((WIN, 128), F32),
            pltpu.VMEM((SPAN, 128), F32),
            pltpu.VMEM((6, SPAN, 128), BF16),
            pltpu.VMEM((12, ROWS, 128), BF16),
            pltpu.VMEM((2, 8, 128), F32),
            pltpu.VMEM((2, 32, 8, 128), F32),
            pltpu.VMEM((2, 8, 128), F32),
            pltpu.VMEM((16, 128), F32),
            pltpu.VMEM((2, 16, 8, 128), F32),
            pltpu.VMEM((2, 16, 128), F32),
            pltpu.VMEM((2, 8, 128), F32),
            pltpu.VMEM((8, 128), F32),
            pltpu.VMEM((ROWS, D), BF16),
            dma((9,)),
            dma((SENDS,)),
            dma((len(NAMES),)),
            dma((2, 32)),
            dma((2, 32)),
            dma((2, 16)),
            dma((2, 16)),
        ],
        compiler_params=pltpu.CompilerParams(
            collective_id=0, has_side_effects=True, vmem_limit_bytes=(64 << 20) - (128 << 10)
        ),
    )(
        frames_in, lengths, ln_gain, ln_bias, glu_weight, conv_kernel,
        bn_gain, bn_bias, out_weight,
    )


def solution(mesh):
    return jax.shard_map(
        per_device,
        mesh=mesh,
        in_specs=(
            P("dp", "tensor", None),
            P("dp"),
            P(),
            P(),
            P(None, "tensor", None),
            P(None, "tensor"),
            P("tensor"),
            P("tensor"),
            P("tensor", None),
        ),
        out_specs=P("dp", "tensor", None),
        check_vma=False,
    )
```

```python
import functools

import jax
import jax.numpy as jnp
from jax import lax
from jax.experimental import pallas as pl
from jax.experimental.pallas import tpu as pltpu
from jax.sharding import PartitionSpec as P

MESH = pl.DeviceIdType.MESH
F32 = jnp.float32
BF16 = jnp.bfloat16
TAPS = 32
D = 1536
SHARD = 192
CHIP = 384
ROWS = 128
HALO = 16
SPAN = 2 * ROWS
WIN = SPAN + 2 * HALO
QUARTER = SHARD // 4
CHUNKS = 3
CROWS = QUARTER // CHUNKS
LNS = 2
LROWS = ROWS // LNS
SENDS = 160

NAMES = (
    ["glu_sib", "low", "high", "pack_s", "pack_e", "pack_d", "w_sib"]
    + [f"blk{p}_{i}" for p in range(2) for i in range(LNS)]
    + [f"gy{i}" for i in range(CHUNKS)]
    + [f"gx{k}_{i}" for k in range(3) for i in range(CHUNKS)]
    + [f"gf{k}_{i}" for k in range(4) for i in range(CHUNKS)]
    + ["we", "wp", "wq"]
    + [f"w{s}x{k}" for s in "epq" for k in range(3)]
    + [f"w{s}f{k}" for s in "epq" for k in range(4)]
    + [f"d{k}_{g}" for k in range(2) for g in range(2)]
    + ["ml0", "ml1"]
    + ["gain0", "gain1"]
)
SEM = {name: i for i, name in enumerate(NAMES)}


def body(
    frames, lengths, ln_gain, ln_bias, glu_w, taps_in, bn_gain, bn_bias, out_w, out,
    xin, lng, lnb, tin, bg, bb, own, nbuf, wg, wf, pack, par, gs, cv, dsend, dbuf,
    msg, plane, bmsg, gmsg, ball, gall, mlx, mlm, act,
    lsem, ssem, rsem, asend, arecv, bsend, brecv,
):
    dp = lax.axis_index("dp")
    t = lax.axis_index("tensor")
    x, yh, z = dp // 16, (dp // 8) % 2, dp % 8
    y, c = t // 2, t % 2
    h, j = y // 2, y % 2
    me = yh * 8 + t
    sib = t + 1 - 2 * c
    par_t = (y + 1 - 2 * j) * 2 + c
    ext_t = (3 - y) * 2 + c
    ext_s = (3 - y) * 2 + 1 - c
    edge = (y == 0) | (y == 3)
    ext_dp = jnp.where(edge, dp + 8 - 16 * yh, dp)
    pe_t = (3 - (y + 1 - 2 * j)) * 2 + c

    colour = (x + 2 * z) % 4
    near = [
        ((((x + 1) % 4) * 2 + yh) * 8 + z, (colour + 1) % 4, 1),
        ((((x + 3) % 4) * 2 + yh) * 8 + z, (colour + 3) % 4, 0),
        ((x * 2 + yh) * 8 + z + 1 - 2 * (z % 2), (colour + 2) % 4, 2),
    ]
    sent = []

    def send(src, dst, recv, tensor, to_dp=dp, cond=None):
        copy = pltpu.make_async_remote_copy(
            src_ref=src, dst_ref=dst, send_sem=ssem.at[len(sent)], recv_sem=rsem.at[SEM[recv]],
            device_id={"dp": to_dp, "tensor": tensor}, device_id_type=MESH,
        )
        sent.append((cond, copy))
        if cond is None:
            copy.start()
        else:
            pl.when(cond)(copy.start)

    def arrived(dst, recv):
        pltpu.make_async_remote_copy(
            src_ref=dst, dst_ref=dst, send_sem=ssem.at[0], recv_sem=rsem.at[SEM[recv]],
            device_id={"dp": dp, "tensor": sib}, device_id_type=MESH,
        ).wait_recv()

    barrier = pltpu.get_barrier_semaphore()

    loads = [
        pltpu.make_async_copy(frames.at[0], xin, lsem.at[0]),
        pltpu.make_async_copy(ln_gain, lng, lsem.at[1]),
        pltpu.make_async_copy(ln_bias, lnb, lsem.at[2]),
        pltpu.make_async_copy(taps_in, tin, lsem.at[3]),
        pltpu.make_async_copy(bn_gain, bg, lsem.at[4]),
        pltpu.make_async_copy(bn_bias, bb, lsem.at[5]),
        pltpu.make_async_copy(glu_w, wg.at[h, :, pl.ds(pl.multiple_of(SHARD * c, 64), SHARD)], lsem.at[6]),
        pltpu.make_async_copy(out_w, wf.at[pl.ds(pl.multiple_of(SHARD * t, 64), SHARD)], lsem.at[7]),
    ]
    for copy in loads:
        copy.start()

    def greet_plane(i, _):
        to = (((x + i // 8) % 4) * 2 + yh) * 8 + (z + i % 8) % 8
        pl.semaphore_signal(barrier, inc=1, device_id={"dp": to, "tensor": t}, device_id_type=MESH)
        return 0

    def greet_line(i, _):
        q = (me + i) % 16
        to = (x * 2 + q // 8) * 8 + z
        pl.semaphore_signal(barrier, inc=1, device_id={"dp": to, "tensor": q % 8}, device_id_type=MESH)
        return 0

    lax.fori_loop(1, 16, greet_line, 0)
    lax.fori_loop(1, 32, greet_plane, 0)

    for copy in loads[:3]:
        copy.wait()
    for i in range(LNS):
        at = slice(LROWS * i, LROWS * (i + 1))
        rows = xin[at, :].astype(F32)
        center = jnp.mean(rows, axis=-1, keepdims=True)
        spread = jnp.mean((rows - center) ** 2, axis=-1, keepdims=True)
        own[at, :] = (
            (rows - center) * lax.rsqrt(spread + 1e-05) * lng[...][None, :] + lnb[...][None, :]
        ).astype(BF16)
    pl.semaphore_wait(barrier, 46)

    same = (y + 2 * c - 1) // 2 == h
    gives = ((c == 1) & (y < 3)) | ((c == 0) & (y > 0))
    y2 = y + 2 * c - 1
    h2, j2 = y2 // 2, (y2 + 2) % 2
    mine = j == c

    def glu_rows(slot, core, quarter, i):
        first = SHARD * core + 64 * jnp.where(core == 0, i, 2 - i) + CROWS * quarter
        return wg.at[slot, :, pl.ds(pl.multiple_of(first, 16), CROWS)]

    def w_rows(shard, first=0, n=SHARD):
        return wf.at[pl.ds(pl.multiple_of(SHARD * shard + first, 16), n)]

    def w_quarter(shard, quarter):
        return w_rows(shard, QUARTER * quarter, QUARTER)

    for i in range(CHUNKS):
        first = 64 * jnp.where(c == 0, i, 2 - i) + CROWS * colour
        src = glu_w.at[:, pl.ds(pl.multiple_of(first, 16), CROWS)]
        send(src, glu_rows(h, c, colour, i), f"gy{i}", ext_t, ext_dp)
    send(glu_w, wg.at[h, :, pl.ds(pl.multiple_of(SHARD * c, 64), SHARD)], "glu_sib", sib)

    away = jnp.logical_not(mine)
    for i in range(LNS):
        at = slice(LROWS * i, LROWS * (i + 1))
        spot = nbuf.at[pl.ds(pl.multiple_of(HALO + ROWS * c + LROWS * i, 16), LROWS)]
        for core in range(2):
            send(own.at[at], spot, f"blk{core}_{i}", (y + 1 - 2 * j) * 2 + j, cond=c == core)
            send(own.at[at], spot, f"blk{core}_{i}", sib, cond=(c == core) & away)

    low = nbuf.at[0:HALO]
    high = nbuf.at[WIN - HALO : WIN]
    tail = own.at[ROWS - HALO : ROWS]
    head = own.at[0:HALO]
    halo_a = jnp.where(same, par_t, (2 * h2) * 2 + j2)
    halo_b = (2 * h2 + 1) * 2 + j2
    apart = jnp.logical_not(same)
    send(tail, low, "low", halo_a, cond=(c == 1) & gives)
    send(tail, low, "low", halo_b, cond=(c == 1) & gives & apart)
    send(head, high, "high", halo_a, cond=(c == 0) & gives)
    send(head, high, "high", halo_b, cond=(c == 0) & gives & apart)

    for copy in loads[3:6]:
        copy.wait()
    pack[0] = jnp.zeros_like(pack[0])
    pack[0, 0:TAPS, 0:SHARD] = tin[...].astype(F32)
    pack[0, TAPS : TAPS + 1, 0:SHARD] = bg[...][None, :]
    pack[0, TAPS + 1 : TAPS + 2, 0:SHARD] = bb[...][None, :]
    send(pack.at[0], pack.at[1], "pack_s", sib)
    send(pack.at[0], pack.at[2], "pack_e", ext_t, ext_dp)

    @pl.when(mine)
    def _():
        nbuf[pl.ds(pl.multiple_of(HALO + ROWS * c, 16), ROWS), :] = own[...]

    @pl.when((c == 1) & (j == 0))
    def _():
        nbuf[0:HALO, :] = own[ROWS - HALO : ROWS, :]

    @pl.when((c == 0) & (j == 1))
    def _():
        nbuf[WIN - HALO : WIN, :] = own[0:HALO, :]

    @pl.when((c == 0) & (h == 0))
    def _():
        nbuf[0:HALO, :] = jnp.zeros((HALO, D), BF16)

    @pl.when((c == 1) & (h == 1))
    def _():
        nbuf[WIN - HALO : WIN, :] = jnp.zeros((HALO, D), BF16)

    lane = lax.broadcasted_iota(jnp.int32, (40, 128), 1)

    def tiles_of(slot, mine_at, other_at):
        a = pack[mine_at]
        b = pack[other_at]
        first = jnp.where(c == 0, a, b)
        second = jnp.where(c == 0, b, a)
        r0 = pltpu.roll(second[:, 0:128], 64, 1)
        r1 = pltpu.roll(second[:, 128:256], 64, 1)
        par[3 * slot] = first[:, 0:128]
        par[3 * slot + 1] = jnp.where(lane < 64, first[:, 128:256], r0)
        par[3 * slot + 2] = jnp.where(lane < 64, r0, r1)

    arrived(pack.at[1], "pack_s")
    tiles_of(h, 0, 1)
    length = lengths[0]
    start = 2 * SPAN * h + SPAN * c
    count = jnp.clip(length - start, 0, SPAN)
    count_f = count.astype(F32)
    inverse = 1.0 / jnp.maximum(count_f, 1.0)
    msg[...] = jnp.zeros_like(msg)
    mlm[...] = jnp.zeros_like(mlm)
    for kind in range(2):
        msg[kind, 6:7, :] = jnp.full((1, 128), count_f, F32)

    def one_tile(slot, q, kind):
        k = 3 * slot + q
        w = wg[slot, :, pl.ds(pl.multiple_of(128 * q, 128), 128), :].reshape(256, D)
        both = lax.dot_general(nbuf[...], w, (((1,), (1,)), ((), ())), preferred_element_type=F32)
        glu = (both[:, 0:128] * jax.nn.sigmoid(both[:, 128:256])).astype(BF16).astype(F32)
        at = lax.broadcasted_iota(jnp.int32, (WIN, 128), 0)
        gs[...] = jnp.where(at < length - start + HALO, glu, 0.0)
        step = 64

        def conv_rows(i, total):
            first = pl.multiple_of(i * step, step)
            acc = jnp.zeros((step, 128), F32)
            for tap in range(TAPS):
                acc = acc + gs[pl.ds(first + (tap + 1), step), :] * par[k, tap : tap + 1, :]
            cv[pl.ds(first, step), :] = acc
            here = first + lax.broadcasted_iota(jnp.int32, (step, 128), 0)
            kept = jnp.where(here < count, acc, 0.0)
            return total + jnp.sum(kept.reshape(step // 8, 8, 128), axis=0)

        total = lax.fori_loop(0, SPAN // step, conv_rows, jnp.zeros((8, 128), F32))
        local = jnp.sum(total, axis=0, keepdims=True) * inverse
        dev = cv[...] - local
        dsend[k] = dev.astype(BF16)
        here = lax.broadcasted_iota(jnp.int32, (SPAN, 128), 0)
        kept = jnp.where(here < count, dev, 0.0)
        mlm[pl.ds(k, 1), :] = local
        msg[kind, q : q + 1, :] = local
        msg[kind, 3 + q : 4 + q, :] = jnp.sum(kept * kept, axis=0, keepdims=True)

    owner = 2 * (2 * h + c)
    shard_of = (jnp.minimum(y, 3 - y), jnp.maximum(y, 3 - y))

    def give(slot, q, n, group):
        base = 3 * jnp.where(slot == 0, shard_of[0], shard_of[1]) + q
        for g in range(2):
            src = dsend.at[pl.ds(3 * slot + q, n), pl.ds(ROWS * g, ROWS)]
            dst = dbuf.at[pl.ds(base, n)]
            kept = mine & (c == g)
            for s in range(2):
                send(src, dst, f"d{group}_{s}", owner + g, cond=jnp.logical_not(kept) & (j == s))

            @pl.when(kept)
            def _(src=src, dst=dst):
                keep = pltpu.make_async_copy(src, dst, lsem.at[8])
                keep.start()
                keep.wait()

    w_mine = out_w.at[pl.ds(pl.multiple_of(QUARTER * colour, 16), QUARTER)]
    for i in range(CHUNKS):
        at = glu_rows(1 - h, c, colour, i)
        arrived(at, f"gy{i}")
        for to_dp, _, k in near:
            send(at, at, f"gx{k}_{i}", t, to_dp)
        send(at, at, f"gf3_{i}", sib)
        if i == 1:
            send(w_mine, w_quarter(t, colour), "we", ext_t, ext_dp)

    def pass_glu(i):
        for k, (_, their, _) in enumerate(near):
            at = glu_rows(1 - h, c, their, i)
            arrived(at, f"gx{k}_{i}")
            send(at, at, f"gf{k}_{i}", sib)

    def plane_copy(i, kind):
        to = (((x + i // 8) % 4) * 2 + yh) * 8 + (z + i % 8) % 8
        return pltpu.make_async_remote_copy(
            src_ref=msg.at[kind], dst_ref=plane.at[kind, i], send_sem=asend.at[kind, i], recv_sem=arecv.at[kind, i],
            device_id={"dp": to, "tensor": t}, device_id_type=MESH,
        )

    def line_copy(i, kind):
        q = (me + i) % 16
        to = (x * 2 + q // 8) * 8 + z
        return pltpu.make_async_remote_copy(
            src_ref=bmsg.at[kind], dst_ref=ball.at[kind, me], send_sem=bsend.at[kind, i], recv_sem=brecv.at[kind, me],
            device_id={"dp": to, "tensor": q % 8}, device_id_type=MESH,
        )

    def over(order, what):
        for i in order:
            what(i)

    def merge(blocks):
        n = sum(jnp.broadcast_to(b[6:7, :], (8, 128)) for b in blocks)
        mean = sum(jnp.broadcast_to(b[6:7, :], (8, 128)) * b for b in blocks) / jnp.maximum(n, 1.0)
        apart = sum(jnp.broadcast_to(b[6:7, :], (8, 128)) * (b - mean) ** 2 for b in blocks)
        return n, mean, sum(blocks) + pltpu.roll(apart, 3, 0)

    row = lax.broadcasted_iota(jnp.int32, (8, 128), 0)
    plane_order = sorted(range(1, 32), key=lambda i: -min(i // 8, 4 - i // 8) - min(i % 8, 8 - i % 8))
    line_order = sorted(range(1, 16), key=lambda i: -min(i, 16 - i))

    def send_plane(kind):
        over(plane_order, lambda i: plane_copy(i, kind).start())
        plane[kind, 0] = msg[kind]

    def plane_to_line(kind):
        over(plane_order, lambda i: plane_copy(i, kind).wait_recv())
        n, mean, square = merge([plane[kind, i] for i in range(32)])
        bmsg[kind] = jnp.where(row < 3, mean, jnp.where(row == 6, n, square))
        over(line_order, lambda i: line_copy(i, kind).start())
        ball[kind, me] = bmsg[kind]

    for p in range(2):
        @pl.when(jnp.logical_not(mine & (c == p)))
        def _(p=p):
            for i in range(LNS):
                first = HALO + ROWS * p + LROWS * i
                arrived(nbuf.at[first : first + LROWS], f"blk{p}_{i}")

    @pl.when(((c == 1) & (j == 1)) | ((c == 0) & (h == 1)))
    def _():
        arrived(low, "low")

    @pl.when(((c == 0) & (j == 0)) | ((c == 1) & (h == 0)))
    def _():
        arrived(high, "high")

    loads[6].wait()
    arrived(wg.at[h, :, pl.ds(pl.multiple_of(SHARD * (1 - c), 64), SHARD)], "glu_sib")

    send(w_mine, w_quarter(t, colour), "wp", par_t)
    send(out_w, w_rows(t), "w_sib", sib)

    w_from = {"e": ext_t, "p": par_t, "q": pe_t}

    def w_on(s):
        at = w_quarter(w_from[s], colour)
        arrived(at, f"w{s}")
        if s == "e":
            send(at, at, "wq", par_t)
        for to_dp, _, k in near:
            send(at, at, f"w{s}x{k}", t, to_dp)
        send(at, at, f"w{s}f3", sib)

    def w_last(s):
        for k, (_, their, _) in enumerate(near):
            at = w_quarter(w_from[s], their)
            arrived(at, f"w{s}x{k}")
            send(at, at, f"w{s}f{k}", sib)

    one_tile(h, 0, 0)
    pass_glu(0)
    w_on("e")
    arrived(pack.at[2], "pack_e")
    send(pack.at[2], pack.at[3], "pack_d", sib)
    one_tile(h, 1, 0)
    pass_glu(1)
    one_tile(h, 2, 0)
    pass_glu(2)
    send_plane(0)
    give(h, 0, 3, 0)

    arrived(pack.at[3], "pack_d")
    tiles_of(1 - h, 2, 3)
    quarters = [their for _, their, _ in near] + [colour]

    def glu_arrived(i):
        for k in range(4):
            arrived(glu_rows(1 - h, 1 - c, quarters[k], i), f"gf{k}_{i}")

    glu_arrived(0)
    glu_arrived(1)
    one_tile(1 - h, 0, 1)
    one_tile(1 - h, 2, 1)
    glu_arrived(2)
    one_tile(1 - h, 1, 1)
    send_plane(1)
    give(1 - h, 0, 3, 1)
    u = jnp.where(edge, 0, 1)
    for g in range(2):
        for s in range(2):
            send(mlm, mlx.at[s], f"ml{s}", owner + g, cond=jnp.logical_not(mine & (c == g)) & (u == s))

    @pl.when(mine)
    def _():
        mlx[u] = mlm[...]

    gmsg[...] = jnp.zeros_like(gmsg)
    for k in range(6):
        gmsg[k : k + 1, :] = par[k, TAPS : TAPS + 1, :]
        gmsg[8 + k : 9 + k, :] = par[k, TAPS + 1 : TAPS + 2, :]
    for giver in range(2):
        is_giver = t == 2 * giver
        for i in range(1, 8):
            send(gmsg, gall.at[giver], f"gain{giver}", (t + i) % 8, cond=is_giver)

        @pl.when(is_giver)
        def _(giver=giver):
            gall[giver] = gmsg[...]

    w_last("e")
    plane_to_line(0)
    w_on("p")
    plane_to_line(1)
    w_on("q")
    w_last("p")
    w_last("q")

    def line_arrived(i):
        q = (me + i) % 16
        for kind in range(2):
            pltpu.make_async_remote_copy(
                src_ref=bmsg.at[kind], dst_ref=ball.at[kind, q], send_sem=bsend.at[0, 0], recv_sem=brecv.at[kind, q],
                device_id={"dp": dp, "tensor": sib}, device_id_type=MESH,
            ).wait_recv()

    for group, n in ((0, 3), (1, 3)):
        for s in range(2):
            @pl.when(jnp.logical_not((j == s) & mine))
            def _(group=group, n=n, s=s):
                arrived(dbuf.at[pl.ds(0, n)], f"d{group}_{s}")
    for s in range(2):
        @pl.when(jnp.logical_not((u == s) & mine))
        def _(s=s):
            arrived(mlx.at[s], f"ml{s}")

    for giver in range(2):
        @pl.when(t != 2 * giver)
        def _(giver=giver):
            arrived(gall.at[giver], f"gain{giver}")

    over(line_order, line_arrived)
    for shard in range(4):
        from_own = [ball[0, 8 * g + 2 * shard + core] for g in range(2) for core in range(2)]
        from_extra = [ball[1, 8 * g + 2 * (3 - shard) + core] for g in range(2) for core in range(2)]
        n, mean, square = merge(from_own + from_extra)
        n1 = jnp.broadcast_to(n[0:1, :], (8, 128))
        pair = (0, 1, 1, 0)[shard]
        first = 3 * (shard // 2)
        root = lax.rsqrt(square / n1 + 1e-05)
        for r in range(3):
            g = 3 * shard + r
            k = first + r
            scale = root[3 + r : 4 + r, :] * gall[pair, k : k + 1, :]
            offset = mlx[pair, k : k + 1, :] - mean[r : r + 1, :]
            zed = (dbuf[g].astype(F32) + offset) * scale + gall[pair, 8 + k : 9 + k, :]
            act[:, 128 * g : 128 * (g + 1)] = (zed * jax.nn.sigmoid(zed)).astype(BF16)

    def columns(chip):
        at = pl.multiple_of(CHIP * chip, 128)
        branch = lax.dot_general(
            act[...], wf[pl.ds(at, CHIP), :], (((1,), (1,)), ((), ())), preferred_element_type=F32
        )
        out[0, :, pl.ds(at, CHIP)] = (xin[:, pl.ds(at, CHIP)].astype(F32) + branch).astype(BF16)

    loads[7].wait()
    arrived(w_rows(sib), "w_sib")
    columns(y)
    for s in "epq":
        for k in range(4):
            arrived(w_quarter(w_from[s] + 1 - 2 * c, quarters[k]), f"w{s}f{k}")
        columns(w_from[s] // 2)

    for cond, copy in sent:
        if cond is None:
            copy.wait_send()
        else:
            pl.when(cond)(copy.wait_send)

    for kind in range(2):
        over(plane_order, lambda i, kind=kind: plane_copy(i, kind).wait_send())
        over(line_order, lambda i, kind=kind: line_copy(i, kind).wait_send())


def per_device(
    frames_in, lengths, ln_gain, ln_bias, glu_weight, conv_kernel, bn_gain, bn_bias, out_weight
):
    hbm = pl.BlockSpec(memory_space=pltpu.HBM)
    dma = pltpu.SemaphoreType.DMA
    far = functools.partial(pltpu.with_memory_space_constraint, memory_space=pltpu.HBM)
    return pl.pallas_call(
        body,
        out_shape=jax.ShapeDtypeStruct((1, ROWS, D), BF16),
        in_specs=[hbm, pl.BlockSpec(memory_space=pltpu.SMEM)] + [hbm] * 7,
        out_specs=pl.BlockSpec(memory_space=pltpu.VMEM),
        scratch_shapes=[
            pltpu.VMEM((ROWS, D), BF16),
            pltpu.VMEM((D,), F32),
            pltpu.VMEM((D,), F32),
            pltpu.VMEM((TAPS, SHARD), BF16),
            pltpu.VMEM((SHARD,), F32),
            pltpu.VMEM((SHARD,), F32),
            pltpu.VMEM((ROWS, D), BF16),
            pltpu.VMEM((WIN, D), BF16),
            pltpu.VMEM((2, 2, CHIP, D), BF16),
            pltpu.VMEM((D, D), BF16),
            pltpu.VMEM((4, 40, 256), F32),
            pltpu.VMEM((6, 40, 128), F32),
            pltpu.VMEM((WIN, 128), F32),
            pltpu.VMEM((SPAN, 128), F32),
            pltpu.VMEM((6, SPAN, 128), BF16),
            pltpu.VMEM((12, ROWS, 128), BF16),
            pltpu.VMEM((2, 8, 128), F32),
            pltpu.VMEM((2, 32, 8, 128), F32),
            pltpu.VMEM((2, 8, 128), F32),
            pltpu.VMEM((16, 128), F32),
            pltpu.VMEM((2, 16, 8, 128), F32),
            pltpu.VMEM((2, 16, 128), F32),
            pltpu.VMEM((2, 8, 128), F32),
            pltpu.VMEM((8, 128), F32),
            pltpu.VMEM((ROWS, D), BF16),
            dma((9,)),
            dma((SENDS,)),
            dma((len(NAMES),)),
            dma((2, 32)),
            dma((2, 32)),
            dma((2, 16)),
            dma((2, 16)),
        ],
        compiler_params=pltpu.CompilerParams(
            collective_id=0, has_side_effects=True, vmem_limit_bytes=48 << 20
        ),
    )(
        far(frames_in), lengths, far(ln_gain), far(ln_bias), far(glu_weight), far(conv_kernel),
        far(bn_gain), far(bn_bias), far(out_weight),
    )


def solution(mesh):
    return jax.shard_map(
        per_device,
        mesh=mesh,
        in_specs=(
            P("dp", "tensor", None),
            P("dp"),
            P(),
            P(),
            P(None, "tensor", None),
            P(None, "tensor"),
            P("tensor"),
            P("tensor"),
            P("tensor", None),
        ),
        out_specs=P("dp", "tensor", None),
        check_vma=False,
    )
```

```python
import functools

import jax
import jax.numpy as jnp
from jax import lax
from jax.experimental import pallas as pl
from jax.experimental.pallas import tpu as pltpu
from jax.sharding import PartitionSpec as P

MESH = pl.DeviceIdType.MESH
F32 = jnp.float32
BF16 = jnp.bfloat16
TAPS = 32
D = 1536
SHARD = 192
CHIP = 384
ROWS = 128
HALO = 16
SPAN = 2 * ROWS
WIN = SPAN + 2 * HALO
QUARTER = SHARD // 4
CHUNKS = 3
CROWS = QUARTER // CHUNKS
LNS = 2
LROWS = ROWS // LNS
SENDS = 160

NAMES = (
    ["glu_sib", "low", "high", "pack_s", "pack_e", "pack_d", "w_sib"]
    + [f"blk{p}_{i}" for p in range(2) for i in range(LNS)]
    + [f"gy{i}" for i in range(CHUNKS)]
    + [f"gx{k}_{i}" for k in range(3) for i in range(CHUNKS)]
    + [f"gf{k}_{i}" for k in range(4) for i in range(CHUNKS)]
    + ["we", "wp", "wq"]
    + [f"w{s}x{k}" for s in "epq" for k in range(3)]
    + [f"w{s}f{k}" for s in "epq" for k in range(4)]
    + [f"d{k}_{g}" for k in range(2) for g in range(2)]
    + ["ml0", "ml1"]
    + ["gain0", "gain1"]
)
SEM = {name: i for i, name in enumerate(NAMES)}


def body(
    frames, lengths, ln_gain, ln_bias, glu_w, taps_in, bn_gain, bn_bias, out_w, out,
    xin, lng, lnb, tin, bg, bb, own, nbuf, wg, wf, pack, par, gs, cv, dsend, dbuf,
    msg, plane, bmsg, gmsg, ball, gall, mlx, mlm, act,
    lsem, ssem, rsem, asend, arecv, bsend, brecv,
):
    dp = lax.axis_index("dp")
    t = lax.axis_index("tensor")
    x, yh, z = dp // 16, (dp // 8) % 2, dp % 8
    y, c = t // 2, t % 2
    h, j = y // 2, y % 2
    me = yh * 8 + t
    sib = t + 1 - 2 * c
    par_t = (y + 1 - 2 * j) * 2 + c
    ext_t = (3 - y) * 2 + c
    ext_s = (3 - y) * 2 + 1 - c
    edge = (y == 0) | (y == 3)
    ext_dp = jnp.where(edge, dp + 8 - 16 * yh, dp)
    pe_t = (3 - (y + 1 - 2 * j)) * 2 + c

    colour = (x + 2 * z) % 4
    near = [
        ((((x + 1) % 4) * 2 + yh) * 8 + z, (colour + 1) % 4, 1),
        ((((x + 3) % 4) * 2 + yh) * 8 + z, (colour + 3) % 4, 0),
        ((x * 2 + yh) * 8 + z + 1 - 2 * (z % 2), (colour + 2) % 4, 2),
    ]
    sent = []

    def send(src, dst, recv, tensor, to_dp=dp, cond=None):
        copy = pltpu.make_async_remote_copy(
            src_ref=src, dst_ref=dst, send_sem=ssem.at[len(sent)], recv_sem=rsem.at[SEM[recv]],
            device_id={"dp": to_dp, "tensor": tensor}, device_id_type=MESH,
        )
        sent.append((cond, copy))
        if cond is None:
            copy.start()
        else:
            pl.when(cond)(copy.start)

    def arrived(dst, recv):
        pltpu.make_async_remote_copy(
            src_ref=dst, dst_ref=dst, send_sem=ssem.at[0], recv_sem=rsem.at[SEM[recv]],
            device_id={"dp": dp, "tensor": sib}, device_id_type=MESH,
        ).wait_recv()

    barrier = pltpu.get_barrier_semaphore()

    loads = [
        pltpu.make_async_copy(frames.at[0], xin, lsem.at[0]),
        pltpu.make_async_copy(ln_gain, lng, lsem.at[1]),
        pltpu.make_async_copy(ln_bias, lnb, lsem.at[2]),
        pltpu.make_async_copy(taps_in, tin, lsem.at[3]),
        pltpu.make_async_copy(bn_gain, bg, lsem.at[4]),
        pltpu.make_async_copy(bn_bias, bb, lsem.at[5]),
        pltpu.make_async_copy(glu_w, wg.at[h, :, pl.ds(pl.multiple_of(SHARD * c, 64), SHARD)], lsem.at[6]),
        pltpu.make_async_copy(out_w, wf.at[pl.ds(pl.multiple_of(SHARD * t, 64), SHARD)], lsem.at[7]),
    ]
    for copy in loads:
        copy.start()

    def greet_plane(i, _):
        to = (((x + i // 8) % 4) * 2 + yh) * 8 + (z + i % 8) % 8
        pl.semaphore_signal(barrier, inc=1, device_id={"dp": to, "tensor": t}, device_id_type=MESH)
        return 0

    def greet_line(i, _):
        q = (me + i) % 16
        to = (x * 2 + q // 8) * 8 + z
        pl.semaphore_signal(barrier, inc=1, device_id={"dp": to, "tensor": q % 8}, device_id_type=MESH)
        return 0

    lax.fori_loop(1, 16, greet_line, 0)
    lax.fori_loop(1, 32, greet_plane, 0)

    for copy in loads[:3]:
        copy.wait()
    for i in range(LNS):
        at = slice(LROWS * i, LROWS * (i + 1))
        rows = xin[at, :].astype(F32)
        center = jnp.mean(rows, axis=-1, keepdims=True)
        spread = jnp.mean((rows - center) ** 2, axis=-1, keepdims=True)
        own[at, :] = (
            (rows - center) * lax.rsqrt(spread + 1e-05) * lng[...][None, :] + lnb[...][None, :]
        ).astype(BF16)
    pl.semaphore_wait(barrier, 46)

    same = (y + 2 * c - 1) // 2 == h
    gives = ((c == 1) & (y < 3)) | ((c == 0) & (y > 0))
    y2 = y + 2 * c - 1
    h2, j2 = y2 // 2, (y2 + 2) % 2
    mine = j == c

    def glu_rows(slot, core, quarter, i):
        first = SHARD * core + 64 * jnp.where(core == 0, i, 2 - i) + CROWS * quarter
        return wg.at[slot, :, pl.ds(pl.multiple_of(first, 16), CROWS)]

    def w_rows(shard, first=0, n=SHARD):
        return wf.at[pl.ds(pl.multiple_of(SHARD * shard + first, 16), n)]

    def w_quarter(shard, quarter):
        return w_rows(shard, QUARTER * quarter, QUARTER)

    for i in range(CHUNKS):
        first = 64 * jnp.where(c == 0, i, 2 - i) + CROWS * colour
        src = glu_w.at[:, pl.ds(pl.multiple_of(first, 16), CROWS)]
        send(src, glu_rows(h, c, colour, i), f"gy{i}", ext_t, ext_dp)
    send(glu_w, wg.at[h, :, pl.ds(pl.multiple_of(SHARD * c, 64), SHARD)], "glu_sib", sib)

    away = jnp.logical_not(mine)
    for i in range(LNS):
        at = slice(LROWS * i, LROWS * (i + 1))
        spot = nbuf.at[pl.ds(pl.multiple_of(HALO + ROWS * c + LROWS * i, 16), LROWS)]
        for core in range(2):
            send(own.at[at], spot, f"blk{core}_{i}", (y + 1 - 2 * j) * 2 + j, cond=c == core)
            send(own.at[at], spot, f"blk{core}_{i}", sib, cond=(c == core) & away)

    low = nbuf.at[0:HALO]
    high = nbuf.at[WIN - HALO : WIN]
    tail = own.at[ROWS - HALO : ROWS]
    head = own.at[0:HALO]
    halo_a = jnp.where(same, par_t, (2 * h2) * 2 + j2)
    halo_b = (2 * h2 + 1) * 2 + j2
    apart = jnp.logical_not(same)
    send(tail, low, "low", halo_a, cond=(c == 1) & gives)
    send(tail, low, "low", halo_b, cond=(c == 1) & gives & apart)
    send(head, high, "high", halo_a, cond=(c == 0) & gives)
    send(head, high, "high", halo_b, cond=(c == 0) & gives & apart)

    for copy in loads[3:6]:
        copy.wait()
    pack[0] = jnp.zeros_like(pack[0])
    pack[0, 0:TAPS, 0:SHARD] = tin[...].astype(F32)
    pack[0, TAPS : TAPS + 1, 0:SHARD] = bg[...][None, :]
    pack[0, TAPS + 1 : TAPS + 2, 0:SHARD] = bb[...][None, :]
    send(pack.at[0], pack.at[1], "pack_s", sib)
    send(pack.at[0], pack.at[2], "pack_e", ext_t, ext_dp)

    @pl.when(mine)
    def _():
        nbuf[pl.ds(pl.multiple_of(HALO + ROWS * c, 16), ROWS), :] = own[...]

    @pl.when((c == 1) & (j == 0))
    def _():
        nbuf[0:HALO, :] = own[ROWS - HALO : ROWS, :]

    @pl.when((c == 0) & (j == 1))
    def _():
        nbuf[WIN - HALO : WIN, :] = own[0:HALO, :]

    @pl.when((c == 0) & (h == 0))
    def _():
        nbuf[0:HALO, :] = jnp.zeros((HALO, D), BF16)

    @pl.when((c == 1) & (h == 1))
    def _():
        nbuf[WIN - HALO : WIN, :] = jnp.zeros((HALO, D), BF16)

    lane = lax.broadcasted_iota(jnp.int32, (40, 128), 1)

    def tiles_of(slot, mine_at, other_at):
        a = pack[mine_at]
        b = pack[other_at]
        first = jnp.where(c == 0, a, b)
        second = jnp.where(c == 0, b, a)
        r0 = pltpu.roll(second[:, 0:128], 64, 1)
        r1 = pltpu.roll(second[:, 128:256], 64, 1)
        par[3 * slot] = first[:, 0:128]
        par[3 * slot + 1] = jnp.where(lane < 64, first[:, 128:256], r0)
        par[3 * slot + 2] = jnp.where(lane < 64, r0, r1)

    arrived(pack.at[1], "pack_s")
    tiles_of(h, 0, 1)
    length = lengths[0]
    start = 2 * SPAN * h + SPAN * c
    count = jnp.clip(length - start, 0, SPAN)
    count_f = count.astype(F32)
    inverse = 1.0 / jnp.maximum(count_f, 1.0)
    msg[...] = jnp.zeros_like(msg)
    mlm[...] = jnp.zeros_like(mlm)
    for kind in range(2):
        msg[kind, 6:7, :] = jnp.full((1, 128), count_f, F32)

    def one_tile(slot, q, kind):
        k = 3 * slot + q
        w = wg[slot, :, pl.ds(pl.multiple_of(128 * q, 128), 128), :].reshape(256, D)
        both = lax.dot_general(nbuf[...], w, (((1,), (1,)), ((), ())), preferred_element_type=F32)
        glu = (both[:, 0:128] * jax.nn.sigmoid(both[:, 128:256])).astype(BF16).astype(F32)
        at = lax.broadcasted_iota(jnp.int32, (WIN, 128), 0)
        gs[...] = jnp.where(at < length - start + HALO, glu, 0.0)
        step = 128

        def conv_rows(i, total):
            first = pl.multiple_of(i * step, step)
            acc = jnp.zeros((step, 128), F32)
            for tap in range(TAPS):
                acc = acc + gs[pl.ds(first + (tap + 1), step), :] * par[k, tap : tap + 1, :]
            cv[pl.ds(first, step), :] = acc
            here = first + lax.broadcasted_iota(jnp.int32, (step, 128), 0)
            kept = jnp.where(here < count, acc, 0.0)
            return total + jnp.sum(kept.reshape(step // 8, 8, 128), axis=0)

        total = lax.fori_loop(0, SPAN // step, conv_rows, jnp.zeros((8, 128), F32))
        local = jnp.sum(total, axis=0, keepdims=True) * inverse
        dev = cv[...] - local
        dsend[k] = dev.astype(BF16)
        here = lax.broadcasted_iota(jnp.int32, (SPAN, 128), 0)
        kept = jnp.where(here < count, dev, 0.0)
        mlm[pl.ds(k, 1), :] = local
        msg[kind, q : q + 1, :] = local
        msg[kind, 3 + q : 4 + q, :] = jnp.sum(kept * kept, axis=0, keepdims=True)

    owner = 2 * (2 * h + c)
    shard_of = (jnp.minimum(y, 3 - y), jnp.maximum(y, 3 - y))

    def give(slot, q, n, group):
        base = 3 * jnp.where(slot == 0, shard_of[0], shard_of[1]) + q
        for g in range(2):
            src = dsend.at[pl.ds(3 * slot + q, n), pl.ds(ROWS * g, ROWS)]
            dst = dbuf.at[pl.ds(base, n)]
            kept = mine & (c == g)
            for s in range(2):
                send(src, dst, f"d{group}_{s}", owner + g, cond=jnp.logical_not(kept) & (j == s))

            @pl.when(kept)
            def _(src=src, dst=dst):
                keep = pltpu.make_async_copy(src, dst, lsem.at[8])
                keep.start()
                keep.wait()

    w_mine = out_w.at[pl.ds(pl.multiple_of(QUARTER * colour, 16), QUARTER)]
    for i in range(CHUNKS):
        at = glu_rows(1 - h, c, colour, i)
        arrived(at, f"gy{i}")
        for to_dp, _, k in near:
            send(at, at, f"gx{k}_{i}", t, to_dp)
        send(at, at, f"gf3_{i}", sib)
        if i == 1:
            send(w_mine, w_quarter(t, colour), "we", ext_t, ext_dp)

    def pass_glu(i):
        for k, (_, their, _) in enumerate(near):
            at = glu_rows(1 - h, c, their, i)
            arrived(at, f"gx{k}_{i}")
            send(at, at, f"gf{k}_{i}", sib)

    def plane_copy(i, kind):
        to = (((x + i // 8) % 4) * 2 + yh) * 8 + (z + i % 8) % 8
        return pltpu.make_async_remote_copy(
            src_ref=msg.at[kind], dst_ref=plane.at[kind, i], send_sem=asend.at[kind, i], recv_sem=arecv.at[kind, i],
            device_id={"dp": to, "tensor": t}, device_id_type=MESH,
        )

    def line_copy(i, kind):
        q = (me + i) % 16
        to = (x * 2 + q // 8) * 8 + z
        return pltpu.make_async_remote_copy(
            src_ref=bmsg.at[kind], dst_ref=ball.at[kind, me], send_sem=bsend.at[kind, i], recv_sem=brecv.at[kind, me],
            device_id={"dp": to, "tensor": q % 8}, device_id_type=MESH,
        )

    def over(order, what):
        for i in order:
            what(i)

    def merge(blocks):
        n = sum(jnp.broadcast_to(b[6:7, :], (8, 128)) for b in blocks)
        mean = sum(jnp.broadcast_to(b[6:7, :], (8, 128)) * b for b in blocks) / jnp.maximum(n, 1.0)
        apart = sum(jnp.broadcast_to(b[6:7, :], (8, 128)) * (b - mean) ** 2 for b in blocks)
        return n, mean, sum(blocks) + pltpu.roll(apart, 3, 0)

    row = lax.broadcasted_iota(jnp.int32, (8, 128), 0)
    plane_order = sorted(range(1, 32), key=lambda i: -min(i // 8, 4 - i // 8) - min(i % 8, 8 - i % 8))
    line_order = sorted(range(1, 16), key=lambda i: -min(i, 16 - i))

    def send_plane(kind):
        over(plane_order, lambda i: plane_copy(i, kind).start())
        plane[kind, 0] = msg[kind]

    def plane_to_line(kind):
        over(plane_order, lambda i: plane_copy(i, kind).wait_recv())
        n, mean, square = merge([plane[kind, i] for i in range(32)])
        bmsg[kind] = jnp.where(row < 3, mean, jnp.where(row == 6, n, square))
        over(line_order, lambda i: line_copy(i, kind).start())
        ball[kind, me] = bmsg[kind]

    for p in range(2):
        @pl.when(jnp.logical_not(mine & (c == p)))
        def _(p=p):
            for i in range(LNS):
                first = HALO + ROWS * p + LROWS * i
                arrived(nbuf.at[first : first + LROWS], f"blk{p}_{i}")

    @pl.when(((c == 1) & (j == 1)) | ((c == 0) & (h == 1)))
    def _():
        arrived(low, "low")

    @pl.when(((c == 0) & (j == 0)) | ((c == 1) & (h == 0)))
    def _():
        arrived(high, "high")

    loads[6].wait()
    arrived(wg.at[h, :, pl.ds(pl.multiple_of(SHARD * (1 - c), 64), SHARD)], "glu_sib")

    send(w_mine, w_quarter(t, colour), "wp", par_t)
    send(out_w, w_rows(t), "w_sib", sib)

    w_from = {"e": ext_t, "p": par_t, "q": pe_t}

    def w_on(s):
        at = w_quarter(w_from[s], colour)
        arrived(at, f"w{s}")
        if s == "e":
            send(at, at, "wq", par_t)
        for to_dp, _, k in near:
            send(at, at, f"w{s}x{k}", t, to_dp)
        send(at, at, f"w{s}f3", sib)

    def w_last(s):
        for k, (_, their, _) in enumerate(near):
            at = w_quarter(w_from[s], their)
            arrived(at, f"w{s}x{k}")
            send(at, at, f"w{s}f{k}", sib)

    one_tile(h, 0, 0)
    pass_glu(0)
    w_on("e")
    arrived(pack.at[2], "pack_e")
    send(pack.at[2], pack.at[3], "pack_d", sib)
    one_tile(h, 1, 0)
    pass_glu(1)
    one_tile(h, 2, 0)
    pass_glu(2)
    send_plane(0)
    give(h, 0, 3, 0)

    arrived(pack.at[3], "pack_d")
    tiles_of(1 - h, 2, 3)
    quarters = [their for _, their, _ in near] + [colour]

    def glu_arrived(i):
        for k in range(4):
            arrived(glu_rows(1 - h, 1 - c, quarters[k], i), f"gf{k}_{i}")

    glu_arrived(0)
    glu_arrived(1)
    one_tile(1 - h, 0, 1)
    one_tile(1 - h, 2, 1)
    glu_arrived(2)
    one_tile(1 - h, 1, 1)
    send_plane(1)
    give(1 - h, 0, 3, 1)
    u = jnp.where(edge, 0, 1)
    for g in range(2):
        for s in range(2):
            send(mlm, mlx.at[s], f"ml{s}", owner + g, cond=jnp.logical_not(mine & (c == g)) & (u == s))

    @pl.when(mine)
    def _():
        mlx[u] = mlm[...]

    gmsg[...] = jnp.zeros_like(gmsg)
    for k in range(6):
        gmsg[k : k + 1, :] = par[k, TAPS : TAPS + 1, :]
        gmsg[8 + k : 9 + k, :] = par[k, TAPS + 1 : TAPS + 2, :]
    for giver in range(2):
        is_giver = t == 2 * giver
        for i in range(1, 8):
            send(gmsg, gall.at[giver], f"gain{giver}", (t + i) % 8, cond=is_giver)

        @pl.when(is_giver)
        def _(giver=giver):
            gall[giver] = gmsg[...]

    plane_to_line(0)
    w_on("p")
    w_last("e")
    plane_to_line(1)
    w_on("q")
    w_last("p")
    w_last("q")

    def line_arrived(i):
        q = (me + i) % 16
        for kind in range(2):
            pltpu.make_async_remote_copy(
                src_ref=bmsg.at[kind], dst_ref=ball.at[kind, q], send_sem=bsend.at[0, 0], recv_sem=brecv.at[kind, q],
                device_id={"dp": dp, "tensor": sib}, device_id_type=MESH,
            ).wait_recv()

    for group, n in ((0, 3), (1, 3)):
        for s in range(2):
            @pl.when(jnp.logical_not((j == s) & mine))
            def _(group=group, n=n, s=s):
                arrived(dbuf.at[pl.ds(0, n)], f"d{group}_{s}")
    for s in range(2):
        @pl.when(jnp.logical_not((u == s) & mine))
        def _(s=s):
            arrived(mlx.at[s], f"ml{s}")

    for giver in range(2):
        @pl.when(t != 2 * giver)
        def _(giver=giver):
            arrived(gall.at[giver], f"gain{giver}")

    over(line_order, line_arrived)
    for shard in range(4):
        from_own = [ball[0, 8 * g + 2 * shard + core] for g in range(2) for core in range(2)]
        from_extra = [ball[1, 8 * g + 2 * (3 - shard) + core] for g in range(2) for core in range(2)]
        n, mean, square = merge(from_own + from_extra)
        n1 = jnp.broadcast_to(n[0:1, :], (8, 128))
        pair = (0, 1, 1, 0)[shard]
        first = 3 * (shard // 2)
        root = lax.rsqrt(square / n1 + 1e-05)
        for r in range(3):
            g = 3 * shard + r
            k = first + r
            scale = root[3 + r : 4 + r, :] * gall[pair, k : k + 1, :]
            offset = mlx[pair, k : k + 1, :] - mean[r : r + 1, :]
            zed = (dbuf[g].astype(F32) + offset) * scale + gall[pair, 8 + k : 9 + k, :]
            act[:, 128 * g : 128 * (g + 1)] = (zed * jax.nn.sigmoid(zed)).astype(BF16)

    def columns(chip):
        at = pl.multiple_of(CHIP * chip, 128)
        branch = lax.dot_general(
            act[...], wf[pl.ds(at, CHIP), :], (((1,), (1,)), ((), ())), preferred_element_type=F32
        )
        out[0, :, pl.ds(at, CHIP)] = (xin[:, pl.ds(at, CHIP)].astype(F32) + branch).astype(BF16)

    loads[7].wait()
    arrived(w_rows(sib), "w_sib")
    columns(y)
    for s in "epq":
        for k in range(4):
            arrived(w_quarter(w_from[s] + 1 - 2 * c, quarters[k]), f"w{s}f{k}")
        columns(w_from[s] // 2)

    for cond, copy in sent:
        if cond is None:
            copy.wait_send()
        else:
            pl.when(cond)(copy.wait_send)

    for kind in range(2):
        over(plane_order, lambda i, kind=kind: plane_copy(i, kind).wait_send())
        over(line_order, lambda i, kind=kind: line_copy(i, kind).wait_send())


def per_device(
    frames_in, lengths, ln_gain, ln_bias, glu_weight, conv_kernel, bn_gain, bn_bias, out_weight
):
    hbm = pl.BlockSpec(memory_space=pltpu.HBM)
    dma = pltpu.SemaphoreType.DMA
    far = functools.partial(pltpu.with_memory_space_constraint, memory_space=pltpu.HBM)
    return pl.pallas_call(
        body,
        out_shape=jax.ShapeDtypeStruct((1, ROWS, D), BF16),
        in_specs=[hbm, pl.BlockSpec(memory_space=pltpu.SMEM)] + [hbm] * 7,
        out_specs=pl.BlockSpec(memory_space=pltpu.VMEM),
        scratch_shapes=[
            pltpu.VMEM((ROWS, D), BF16),
            pltpu.VMEM((D,), F32),
            pltpu.VMEM((D,), F32),
            pltpu.VMEM((TAPS, SHARD), BF16),
            pltpu.VMEM((SHARD,), F32),
            pltpu.VMEM((SHARD,), F32),
            pltpu.VMEM((ROWS, D), BF16),
            pltpu.VMEM((WIN, D), BF16),
            pltpu.VMEM((2, 2, CHIP, D), BF16),
            pltpu.VMEM((D, D), BF16),
            pltpu.VMEM((4, 40, 256), F32),
            pltpu.VMEM((6, 40, 128), F32),
            pltpu.VMEM((WIN, 128), F32),
            pltpu.VMEM((SPAN, 128), F32),
            pltpu.VMEM((6, SPAN, 128), BF16),
            pltpu.VMEM((12, ROWS, 128), BF16),
            pltpu.VMEM((2, 8, 128), F32),
            pltpu.VMEM((2, 32, 8, 128), F32),
            pltpu.VMEM((2, 8, 128), F32),
            pltpu.VMEM((16, 128), F32),
            pltpu.VMEM((2, 16, 8, 128), F32),
            pltpu.VMEM((2, 16, 128), F32),
            pltpu.VMEM((2, 8, 128), F32),
            pltpu.VMEM((8, 128), F32),
            pltpu.VMEM((ROWS, D), BF16),
            dma((9,)),
            dma((SENDS,)),
            dma((len(NAMES),)),
            dma((2, 32)),
            dma((2, 32)),
            dma((2, 16)),
            dma((2, 16)),
        ],
        compiler_params=pltpu.CompilerParams(
            collective_id=0, has_side_effects=True, vmem_limit_bytes=48 << 20
        ),
    )(
        far(frames_in), lengths, far(ln_gain), far(ln_bias), far(glu_weight), far(conv_kernel),
        far(bn_gain), far(bn_bias), far(out_weight),
    )


def solution(mesh):
    return jax.shard_map(
        per_device,
        mesh=mesh,
        in_specs=(
            P("dp", "tensor", None),
            P("dp"),
            P(),
            P(),
            P(None, "tensor", None),
            P(None, "tensor"),
            P("tensor"),
            P("tensor"),
            P("tensor", None),
        ),
        out_specs=P("dp", "tensor", None),
        check_vma=False,
    )
```
